32 devices in a mesh: row: 8 (over z, x), col: 4 (over y, core).
Axes of the slice: x: 2, y: 2, z: 4, core: 2. Of those that a mesh axis runs over, the one named last changes fastest.
Arguments:
- momentum: bfloat16 [16384, 16384], P('row', 'col'), may hold values from -16 to 16
- gradient: bfloat16 [16384, 16384], P('row', 'col'), may hold values from -6 to 6
- right_basis: bfloat16 [1024, 16384], P('row', 'col'), may hold values from -1 to 1
Outputs:
- momentum_next: bfloat16 [16384, 16384], P('row', 'col')
- basis_next: float32 [1024, 16384], P('row', 'col')
- update: bfloat16 [16384, 16384], P('row', 'col')
The draws below stay inside these ranges and needn't reach their ends.
All inputs are finite; a program needn't handle non-finite values.
Results may differ from the reference program's by a relative error of at most 0.02.
Values may be sent and summed in bfloat16 or wider, within the bound.
A program may use at most 128 MiB of HBM per device.

```python
import math
import jax
import jax.numpy as jnp
from jax import lax

D = 16384
RANK = 1024


def shared_directions(key):
    values = jax.random.normal(jax.random.fold_in(key, 11), (RANK, D), jnp.float32)
    return jnp.clip(values, -6.0, 6.0) * D ** (-0.5)


def draw_right_basis(key, part):
    return shared_directions(key).astype(jnp.bfloat16)


def draw_momentum(key, part):
    directions = shared_directions(key)
    highest = 4.0
    column_low = 0.6
    column_high = 1.8
    residue = jnp.clip(jax.random.normal(jax.random.fold_in(key, 37), (D, D), jnp.float32), -6.0, 6.0)
    scales = jnp.exp(jax.random.uniform(jax.random.fold_in(key, 41), (RANK,), jnp.float32, minval=0.0, maxval=math.log(highest)))
    coefficients = jax.random.normal(jax.random.fold_in(key, 23), (D, RANK), jnp.float32)
    coefficients = jnp.clip(coefficients, -6.0, 6.0) * scales[None, :] * math.sqrt(D / RANK)
    in_span = jnp.dot(coefficients, directions)
    position = jnp.arange(D, dtype=jnp.float32) / float(D - 1)
    column_scale = column_low * jnp.exp(position * math.log(column_high / column_low))
    return jnp.clip((in_span + residue) * column_scale[None, :], -16.0, 16.0).astype(jnp.bfloat16)


def level_of(own_key, extent, cuts, smallest, high):
    def one(axis_at, blocks):
        draws = jax.random.uniform(jax.random.fold_in(jax.random.fold_in(own_key, 6), axis_at), (blocks,), jnp.float32, smallest / len(cuts), high / len(cuts))
        return jnp.repeat(jnp.exp(draws), extent[axis_at] // blocks).reshape((-1,) + (1,) * (len(extent) - axis_at - 1))

    factor_of = one(*cuts[0])
    for cut in cuts[1:]:
        factor_of = factor_of * one(*cut)
    return factor_of


def centred(stream_key, shape, spread, limit, shards=(), kind=jnp.bfloat16):
    result = jax.random.normal(stream_key, shape, jnp.float32) * spread
    if len(shards) > 0:
        result = level_of(stream_key, shape, shards, -0.22, 0.18) * result
    return jnp.clip(result, min=-limit, max=limit).astype(kind)


def setup_inputs(seed: int = 0) -> dict:
    arg_keys = jax.random.split(jax.random.key(seed), 4)
    return {
        "momentum": draw_momentum(jax.random.fold_in(arg_keys[3], 71), 0),
        "gradient": centred(arg_keys[1], (D, D), 1.0, 6.0, ((0, 8), (1, 4))),
        "right_basis": draw_right_basis(jax.random.fold_in(arg_keys[3], 71), 0),
    }


momentum_decay = 0.95
epsilon = 1e-06

def reference(momentum, gradient, right_basis):
    buffer = (momentum.astype(jnp.float32) + gradient.astype(jnp.float32)).astype(jnp.bfloat16)
    projected = jnp.dot(buffer.astype(jnp.float32), right_basis.T.astype(jnp.float32), preferred_element_type=jnp.float32)
    gram_matrix = jnp.dot(projected.T, projected, precision=lax.Precision.HIGHEST)
    lower_factor = jnp.linalg.cholesky(gram_matrix)
    orthonormal = jax.scipy.linalg.solve_triangular(lower_factor, projected.T, lower=True).T.astype(jnp.bfloat16)
    right_new = jnp.dot(orthonormal.T.astype(jnp.float32), buffer.astype(jnp.float32), preferred_element_type=jnp.float32).astype(jnp.bfloat16)
    right_wide = right_new.astype(jnp.float32)
    inverse_norm = lax.rsqrt(lax.optimization_barrier(jnp.sum(right_wide * right_wide, axis=1, keepdims=True)) + epsilon)
    basis_next = right_wide * inverse_norm
    basis_low = basis_next.astype(jnp.bfloat16)
    feedback = jnp.dot(orthonormal.astype(jnp.float32), right_new.astype(jnp.float32), preferred_element_type=jnp.float32)
    momentum_next = (buffer.astype(jnp.float32) - (1.0 - momentum_decay) * feedback).astype(jnp.bfloat16)
    update_scale = D / math.sqrt(RANK)
    update = (update_scale * jnp.dot(orthonormal.astype(jnp.float32), basis_low.astype(jnp.float32), preferred_element_type=jnp.float32)).astype(jnp.bfloat16)
    return (momentum_next, basis_next, update)
```

```python
import functools
import math

import jax
import jax.numpy as jnp
from jax import lax
from jax.experimental import pallas as pl
from jax.experimental.pallas import tpu as pltpu
from jax.sharding import PartitionSpec as P

D = 16384
RANK = 1024

momentum_decay = 0.95
epsilon = 1e-06

BLOCK = 128
GROUP = 8
PACK = 256

HIGHEST = lax.Precision.HIGHEST


def across(x, column):
    return jnp.broadcast_to(x[:, column : column + 1], (x.shape[0], BLOCK))


def down(x, row):
    return jnp.broadcast_to(x[row : row + 1, :], (GROUP, BLOCK))


def factor_block(block):
    groups = BLOCK // GROUP
    sub = lax.broadcasted_iota(jnp.int32, (GROUP, BLOCK), 0)
    lane = lax.broadcasted_iota(jnp.int32, (GROUP, BLOCK), 1)
    left = [block[GROUP * g : GROUP * (g + 1), :] for g in range(groups)]
    right = [jnp.where(lane == sub + GROUP * g, 1.0, 0.0) for g in range(groups)]
    inverse = []
    for g in range(groups):
        first = GROUP * g
        jordan_left, jordan_right = left[g], right[g]
        columns = [across(jordan_left, first + l) for l in range(GROUP)]
        forward_right, pivots = jordan_right, jnp.ones_like(jordan_left)
        for l in range(GROUP):
            pivot = down(columns[l], l)
            reciprocal = 1.0 / pivot
            mine = sub == l
            column = columns[l]
            row_left, row_right = down(jordan_left, l), down(jordan_right, l)
            forward_right = jnp.where(mine, row_right, forward_right)
            pivots = jnp.where(mine, pivot, pivots)
            row_left, row_right = row_left * reciprocal, row_right * reciprocal
            jordan_left = jnp.where(mine, row_left, jordan_left - column * row_left)
            jordan_right = jnp.where(mine, row_right, jordan_right - column * row_right)
            for m in range(l + 1, GROUP):
                row = down(columns[m], l) * reciprocal
                columns[m] = jnp.where(mine, row, columns[m] - column * row)
        inverse.append(forward_right * lax.rsqrt(pivots))
        rows_left = [down(jordan_left, l) for l in range(GROUP)]
        rows_right = [down(jordan_right, l) for l in range(GROUP)]
        for h in range(g + 1, groups):
            base = left[h]
            new_left, new_right = base, right[h]
            for l in range(GROUP):
                coefficient = across(base, first + l)
                new_left = new_left - coefficient * rows_left[l]
                new_right = new_right - coefficient * rows_right[l]
            left[h], right[h] = new_left, new_right
    return jnp.concatenate(inverse, axis=0)


def plain_factor_kernel(packed_ref, share_ref, ortho_ref, work):
    rank = work.shape[0]
    blocks = rank // BLOCK
    offset = 0
    for i in range(rank // PACK):
        for j in range(i + 1):
            tile = packed_ref[:, offset : offset + PACK]
            offset += PACK
            work[PACK * i : PACK * (i + 1), PACK * j : PACK * (j + 1)] = tile
            if j < i:
                work[PACK * j : PACK * (j + 1), PACK * i : PACK * (i + 1)] = tile.T
    column_block = lax.broadcasted_iota(jnp.int32, (BLOCK, rank), 1) // BLOCK

    def step(k, carry):
        here = pl.ds(pl.multiple_of(k * BLOCK, BLOCK), BLOCK)
        x = factor_block(work[here, here])
        pivot_rows = jnp.dot(x, work[here, :], precision=HIGHEST, preferred_element_type=jnp.float32)
        wide = jnp.concatenate([x] * blocks, axis=1)
        pivot_rows = jnp.where(column_block == k, wide, pivot_rows)
        work[here, :] = pivot_rows

        def below(i, carry):
            there = pl.ds(pl.multiple_of(i * BLOCK, BLOCK), BLOCK)
            panel = lax.dot_general(
                work[there, here], x, (((1,), (1,)), ((), ())),
                precision=HIGHEST, preferred_element_type=jnp.float32,
            )
            work[there, here] = jnp.zeros((BLOCK, BLOCK), jnp.float32)
            work[there, :] = work[there, :] - jnp.dot(
                panel, work[here, :], precision=HIGHEST, preferred_element_type=jnp.float32
            )
            return carry

        lax.fori_loop(k + 1, blocks, below, 0)
        rest = jnp.where(column_block <= k, pivot_rows, 0.0)
        total = jnp.zeros((share_ref.shape[0], BLOCK), jnp.float32)
        for _ in range(3):
            part = rest.astype(jnp.bfloat16)
            rest = rest - part.astype(jnp.float32)
            total = total + lax.dot_general(
                share_ref[...], part, (((1,), (1,)), ((), ())),
                preferred_element_type=jnp.float32,
            )
        ortho_ref[:, here] = total.astype(jnp.bfloat16)
        return carry

    lax.fori_loop(0, blocks, step, 0)


def orthonormalize(row_share, packed):
    rank = row_share.shape[1]
    return pl.pallas_call(
        plain_factor_kernel,
        out_shape=jax.ShapeDtypeStruct(row_share.shape, jnp.bfloat16),
        in_specs=[pl.BlockSpec(memory_space=pltpu.VMEM)] * 2,
        out_specs=pl.BlockSpec(memory_space=pltpu.VMEM),
        scratch_shapes=[pltpu.VMEM((rank, rank), jnp.float32)],
        compiler_params=pltpu.CompilerParams(vmem_limit_bytes=40 * 1024 * 1024),
        name="factor",
    )(packed, row_share)


def packed_gram(share):
    pieces = []
    for i in range(share.shape[1] // PACK):
        pieces.append(
            lax.dot_general(
                share[:, PACK * i : PACK * (i + 1)],
                share[:, : PACK * (i + 1)],
                (((0,), (0,)), ((), ())),
                preferred_element_type=jnp.float32,
            )
        )
    return jnp.concatenate(pieces, axis=1)


def plain_body(momentum, gradient, right_basis):
    buffer = (momentum.astype(jnp.float32) + gradient.astype(jnp.float32)).astype(jnp.bfloat16)
    rank_rows = right_basis.shape[0]
    partial_value = lax.dot_general(
        buffer,
        lax.all_gather(right_basis, "row", axis=0, tiled=True),
        (((1,), (1,)), ((), ())),
        preferred_element_type=jnp.float32,
    )
    row_share = lax.psum_scatter(
        partial_value.astype(jnp.bfloat16), "col", scatter_dimension=0, tiled=True
    )
    packed = lax.psum(packed_gram(row_share), ("row", "col"))
    ortho_share = orthonormalize(row_share, packed)
    orthonormal = lax.all_gather(ortho_share, "col", axis=0, tiled=True)
    right_share = lax.psum_scatter(
        lax.dot_general(
            orthonormal, buffer, (((0,), (0,)), ((), ())), preferred_element_type=jnp.float32
        ).astype(jnp.bfloat16),
        "row",
        scatter_dimension=0,
        tiled=True,
    )
    gathered = lax.all_gather(right_share, "row", axis=0, tiled=True)
    right_wide = right_share.astype(jnp.float32)
    sums = jnp.sum(right_wide * right_wide, axis=1)
    everyone = lax.all_gather(sums, ("row", "col"), axis=0)
    everyone = everyone.reshape(lax.axis_size("row"), lax.axis_size("col"), rank_rows)
    inverse_rows = lax.rsqrt(jnp.sum(everyone, axis=1) + epsilon)
    inverse_norm = inverse_rows.reshape(-1, 1)
    mine = lax.dynamic_index_in_dim(inverse_rows, lax.axis_index("row"), 0, keepdims=False)
    basis_next = right_wide * mine[:, None]
    scaled = (gathered.astype(jnp.float32) * inverse_norm).astype(jnp.bfloat16)
    feedback = jnp.dot(orthonormal, gathered, preferred_element_type=jnp.float32)
    direction = jnp.dot(orthonormal, scaled, preferred_element_type=jnp.float32)
    momentum_next = (buffer.astype(jnp.float32) - (1.0 - momentum_decay) * feedback).astype(
        jnp.bfloat16
    )
    update_scale = D / math.sqrt(RANK)
    update = (update_scale * direction).astype(jnp.bfloat16)
    return (momentum_next, basis_next, update)


MESH = pl.DeviceIdType.MESH
CHUNKS = 4
STACK = 9
F32 = jnp.float32
BF16 = jnp.bfloat16


def remote(src, dst, send_sem, recv_sem, device):
    return pltpu.make_async_remote_copy(
        src_ref=src, dst_ref=dst, send_sem=send_sem, recv_sem=recv_sem,
        device_id=device, device_id_type=MESH,
    )


def places():
    row, col = lax.axis_index("row"), lax.axis_index("col")
    return row, col, row // 2, lax.rem(row, 2), col // 2, lax.rem(col, 2)


def greet(devices):
    barrier = pltpu.get_barrier_semaphore()
    for device in devices:
        pl.semaphore_signal(barrier, inc=1, device_id=device, device_id_type=MESH)
    pl.semaphore_wait(barrier, len(devices))


def nt_dot(a, b):
    return lax.dot_general(a, b, (((1,), (1,)), ((), ())), preferred_element_type=F32)


def project_kernel(
    v_ref, m_hbm, g_hbm, pt_ref, b_hbm,
    buf, basis, m_tile, g_tile, part, core_in, half, y_in,
    load_sem, store_sem, own_send, hop_send, x_send, z_recv, x_recv,
    core_send, core_recv, y_send, y_recv, share_send, share_recv,
):
    row, col, z, x, y, k = places()
    rows = buf.shape[0]
    tile = m_tile.shape[1]
    tiles = rows // tile
    x_peer = (z * 2 + 1 - x, col)
    core_peer = (row, y * 2 + 1 - k)
    y_peer = (row, (1 - y) * 2 + k)
    middle = jnp.logical_and(z > 0, z < 3)
    order = [z, jnp.bitwise_xor(z, 1), jnp.where(z < 2, 2, 1), jnp.where(z < 2, 3, 0)]

    def load(i, slot):
        here = pl.ds(pl.multiple_of(i * tile, tile), tile)
        return (
            pltpu.make_async_copy(m_hbm.at[here], m_tile.at[slot], load_sem.at[0, slot]),
            pltpu.make_async_copy(g_hbm.at[here], g_tile.at[slot], load_sem.at[1, slot]),
        )

    for slot in range(2):
        for copy in load(slot, slot):
            copy.start()
    greet(
        [(lax.rem(z + 1, 4) * 2 + x, col), (lax.rem(z + 2, 4) * 2 + x, col), (lax.rem(z + 3, 4) * 2 + x, col)]
        + [x_peer, core_peer, y_peer]
    )
    own_up = remote(v_ref, basis.at[z, x], own_send.at[0], z_recv.at[z], (jnp.minimum(z + 1, 3) * 2 + x, col))
    own_down = remote(v_ref, basis.at[z, x], own_send.at[1], z_recv.at[z], (jnp.maximum(z - 1, 0) * 2 + x, col))
    own_side = remote(v_ref, basis.at[z, x], x_send.at[z], x_recv.at[z], x_peer)

    @pl.when(z < 3)
    def _():
        own_up.start()

    @pl.when(z > 0)
    def _():
        own_down.start()

    own_side.start()
    basis[z, x] = v_ref[...]

    def build(i, carry):
        slot = lax.rem(i, 2)
        for copy in load(i, slot):
            copy.wait()
        here = pl.ds(pl.multiple_of(i * tile, tile), tile)
        buf[here, :] = (m_tile[slot].astype(F32) + g_tile[slot].astype(F32)).astype(BF16)

        @pl.when(i + 2 < tiles)
        def _():
            for copy in load(i + 2, slot):
                copy.start()

        return carry

    lax.fori_loop(0, tiles, build, 0)
    store = pltpu.make_async_copy(buf, b_hbm, store_sem)
    store.start()

    def hop(s):
        q = order[s]
        target = jnp.where(z == 1, jnp.where(q < z, 2, 0), jnp.where(q < z, 3, 1))
        return remote(basis.at[q, x], basis.at[q, x], hop_send.at[s - 1], z_recv.at[q], (target * 2 + x, col))

    def side(s):
        q = order[s]
        return remote(basis.at[q, x], basis.at[q, x], x_send.at[q], x_recv.at[q], x_peer)

    def take(s):
        hop(s).wait_recv()

        @pl.when(middle)
        def _():
            hop(s).start()

        side(s).start()

    def side_in(s):
        q = order[s]
        remote(basis.at[q, x], basis.at[q, 1 - x], x_send.at[q], x_recv.at[q], x_peer).wait_recv()

    def to_core(s):
        return remote(part.at[s, 1 - k], core_in.at[s], core_send.at[s], core_recv.at[s], core_peer)

    def to_y(s):
        return remote(half.at[s], y_in.at[s], y_send.at[s], y_recv.at[s], y_peer)

    def share(s):
        return remote(pt_ref.at[order[s], k], pt_ref.at[order[s], k], share_send.at[s], share_recv.at[s], core_peer)

    def share_in(s):
        return remote(pt_ref.at[order[s], k], pt_ref.at[order[s], 1 - k], share_send.at[s], share_recv.at[s], core_peer)

    def multiply(s):
        q = order[s]
        width = 512

        def columns(n, carry):
            here = pl.ds(pl.multiple_of(n * width, width), width)
            left = basis[q].reshape(2 * basis.shape[2], basis.shape[3])
            value = nt_dot(left, buf[here, :])
            part[s, :, :, here] = value.astype(BF16).reshape(2, basis.shape[2], width)
            return carry

        lax.fori_loop(0, rows // width, columns, 0)
        to_core(s).start()

    def add_core(s):
        to_core(s).wait_recv()
        half[s] = (part[s, k].astype(F32) + core_in[s].astype(F32)).astype(BF16)
        to_y(s).start()

    def add_y(s):
        to_y(s).wait_recv()
        pt_ref[order[s], k] = (half[s].astype(F32) + y_in[s].astype(F32)).astype(BF16)
        share(s).start()

    take(1)

    @pl.when(middle)
    def _():
        take(2)

    side_in(0)
    multiply(0)

    @pl.when(jnp.logical_not(middle))
    def _():
        take(2)

    add_core(0)

    @pl.when(middle)
    def _():
        take(3)

    side_in(1)
    multiply(1)
    add_y(0)
    add_core(1)

    @pl.when(jnp.logical_not(middle))
    def _():
        take(3)

    side_in(2)
    multiply(2)
    add_y(1)
    add_core(2)
    side_in(3)
    multiply(3)
    add_y(2)
    add_core(3)
    add_y(3)

    @pl.when(z < 3)
    def _():
        own_up.wait_send()

    @pl.when(z > 0)
    def _():
        own_down.wait_send()

    own_side.wait_send()

    @pl.when(middle)
    def _():
        for s in range(1, 4):
            hop(s).wait_send()

    for s in range(1, 4):
        side(s).wait_send()
    for s in range(4):
        to_core(s).wait_send()
        to_y(s).wait_send()
        share(s).wait_send()
        share_in(s).wait_recv()
    store.wait()


def project(v, m, g):
    rows, columns = m.shape
    ranks = v.shape[0]
    dma = pltpu.SemaphoreType.DMA
    vmem = pl.BlockSpec(memory_space=pltpu.VMEM)
    anywhere = pl.BlockSpec(memory_space=pl.ANY)
    return pl.pallas_call(
        project_kernel,
        out_shape=(
            jax.ShapeDtypeStruct((4, 2, ranks, rows), BF16),
            jax.ShapeDtypeStruct((rows, columns), BF16),
        ),
        in_specs=[vmem, anywhere, anywhere],
        out_specs=(vmem, anywhere),
        scratch_shapes=[
            pltpu.VMEM((rows, columns), BF16),
            pltpu.VMEM((4, 2, ranks, columns), BF16),
            pltpu.VMEM((2, 128, columns), BF16),
            pltpu.VMEM((2, 128, columns), BF16),
            pltpu.VMEM((4, 2, ranks, rows), BF16),
            pltpu.VMEM((4, ranks, rows), BF16),
            pltpu.VMEM((4, ranks, rows), BF16),
            pltpu.VMEM((4, ranks, rows), BF16),
            dma((2, 2)), dma, dma((2,)), dma((3,)), dma((4,)), dma((4,)), dma((4,)),
            dma((4,)), dma((4,)), dma((4,)), dma((4,)), dma((4,)), dma((4,)),
        ],
        compiler_params=pltpu.CompilerParams(
            collective_id=1, has_side_effects=True, vmem_limit_bytes=58 * 1024 * 1024
        ),
        cost_estimate=pl.CostEstimate(flops=2 * rows * columns * ranks * 8, bytes_accessed=6 * rows * columns, transcendentals=0),
        name="project",
    )(v, m, g)


def factor_kernel(
    pt_ref, b_hbm, ot_ref, n_hbm, sums_ref,
    buf, wpart, x_in, z_in, whole, stack, stack_in, stack_all, work, inverse, squares, norm_in,
    load_sem, store_sem, xs, xr, zs, zr, gs, gr, fs, ys, yr,
    ss, sr, ts, tr, us, ur, ns, nr,
):
    row, col, z, x, y, k = places()
    ranks = pt_ref.shape[2]
    rank = work.shape[0]
    blocks = rank // BLOCK
    chunks = wpart.shape[0]
    width = wpart.shape[4]
    slice_rows = stack_in.shape[1]
    x_peer = (z * 2 + 1 - x, col)
    core_peer = (row, y * 2 + 1 - k)
    y_peer = (row, (1 - y) * 2 + k)

    def z_of(shift):
        return lax.rem(z + shift, 4)

    def z_peer(shift):
        return (z_of(shift) * 2 + x, col)

    def row_of(shift):
        return lax.rem(row + shift, 8)

    def load(j):
        return pltpu.make_async_copy(
            b_hbm.at[:, pl.ds(j * width, width)], buf.at[j % 2], load_sem.at[j % 2]
        )

    load(0).start()
    load(1).start()
    greet([(row_of(shift), col) for shift in range(1, 8)] + [core_peer, y_peer])

    def gram(t, carry):
        early = t < 8 - col
        i = jnp.where(early, col + t, t - 1)
        j = jnp.where(early, col, 7 - col)
        value = nt_dot(pt_ref[i // 2, lax.rem(i, 2)], pt_ref[j // 2, lax.rem(j, 2)])
        stack[pl.ds(pl.multiple_of(t * BLOCK, BLOCK), BLOCK), :] = value
        return carry

    lax.fori_loop(0, STACK, gram, 0)

    def part_of(r):
        return pl.ds(pl.multiple_of(r * slice_rows, slice_rows), slice_rows)

    def gram_out(shift):
        to = row_of(shift)
        return remote(stack.at[part_of(to)], stack_in.at[row], ss.at[shift], sr.at[row], (to, col))

    def gram_in(shift):
        who = row_of(shift)
        return remote(stack.at[part_of(row)], stack_in.at[who], ss.at[shift], sr.at[who], (who, col))

    def sum_out(shift):
        to = row_of(shift)
        return remote(stack_all.at[col, part_of(row)], stack_all.at[col, part_of(row)], ts.at[shift], tr.at[row], (to, col))

    def sum_in(shift):
        who = row_of(shift)
        return remote(stack_all.at[col, part_of(who)], stack_all.at[col, part_of(who)], ts.at[shift], tr.at[who], (who, col))

    def spread(index, what, device):
        return remote(stack_all.at[what], stack_all.at[what], us.at[index], ur.at[index], device)

    for shift in range(1, 8):
        gram_out(shift).start()

    def side_out(j):
        return remote(wpart.at[j, :, 1 - x], x_in.at[j], xs.at[j], xr.at[j], x_peer)

    def weigh(j, which):
        step = 256

        def columns(n, carry):
            here = pl.ds(pl.multiple_of(n * step, step), step)
            left = pt_ref[:, which].reshape(4 * ranks, pt_ref.shape[3])
            value = jnp.dot(left, buf[j % 2, :, here], preferred_element_type=F32)
            wpart[j, :, which, :, here] = value.astype(BF16).reshape(4, ranks, step)
            return carry

        lax.fori_loop(0, width // step, columns, 0)

    def product(j):
        load(j).wait()
        weigh(j, 1 - x)
        side_out(j).start()
        weigh(j, x)
        if j + 2 < chunks:
            load(j + 2).start()

    def line_out(j, shift):
        return remote(x_in.at[j, z_of(shift)], z_in.at[j, z], zs.at[j, shift], zr.at[j, z], z_peer(shift))

    def line_in(j, shift):
        who = z_of(shift)
        return remote(x_in.at[j, who], z_in.at[j, who], zs.at[j, shift], zr.at[j, who], z_peer(shift))

    def add_side(j):
        side_out(j).wait_recv()
        for shift in (1, 2, 3, 0):
            there = z_of(shift)
            x_in[j, there] = (wpart[j, there, x].astype(F32) + x_in[j, there].astype(F32)).astype(BF16)
            if shift:
                line_out(j, shift).start()

    def full_out(j, shift):
        return remote(whole.at[j, z, x], whole.at[j, z, x], gs.at[j, shift], gr.at[j, z], z_peer(shift))

    def full_in(j, shift):
        who = z_of(shift)
        return remote(whole.at[j, who, x], whole.at[j, who, x], gs.at[j, shift], gr.at[j, who], z_peer(shift))

    def full_side(j, shift):
        who = z_of(shift)
        return remote(whole.at[j, who, x], whole.at[j, who, x], fs.at[j, who], ys.at[j, who], x_peer)

    def full_side_in(j, shift):
        who = z_of(shift)
        return remote(whole.at[j, who, x], whole.at[j, who, 1 - x], fs.at[j, who], ys.at[j, who], x_peer)

    def add_line(j):
        total = x_in[j, z].astype(F32)
        for shift in (1, 2, 3):
            line_in(j, shift).wait_recv()
            total = total + z_in[j, z_of(shift)].astype(F32)
        whole[j, z, x] = total.astype(BF16)
        for shift in (1, 2, 3):
            full_out(j, shift).start()
        full_side(j, 0).start()

    def forward(j):
        for shift in (1, 3, 2):
            full_in(j, shift).wait_recv()
            full_side(j, shift).start()

    product(0)
    product(1)
    product(2)
    total = stack[part_of(row), :]
    for shift in range(1, 8):
        gram_in(shift).wait_recv()
        total = total + stack_in[row_of(shift)]
    stack_all[col, part_of(row), :] = total
    for shift in range(1, 8):
        sum_out(shift).start()
    product(3)
    add_side(0)
    for shift in range(1, 8):
        sum_in(shift).wait_recv()
    other_col = (1 - y) * 2 + k
    spread(0, col, core_peer).start()
    spread(1, col, y_peer).start()
    add_side(1)
    spread(1, other_col, y_peer).wait_recv()
    spread(2, other_col, core_peer).start()
    spread(0, y * 2 + 1 - k, core_peer).wait_recv()
    spread(2, (1 - y) * 2 + 1 - k, core_peer).wait_recv()

    for c in range(4):
        for t in range(STACK):
            i, j = (c + t, c) if t < 8 - c else (t - 1, 7 - c)
            value = stack_all[c, BLOCK * t : BLOCK * (t + 1), :]
            work[BLOCK * i : BLOCK * (i + 1), BLOCK * j : BLOCK * (j + 1)] = value
            if i != j:
                work[BLOCK * j : BLOCK * (j + 1), BLOCK * i : BLOCK * (i + 1)] = value.T

    column_block = lax.broadcasted_iota(jnp.int32, (BLOCK, rank), 1) // BLOCK
    events = {
        0: [(add_line, 0)],
        1: [(add_side, 2), (forward, 0)],
        2: [(add_line, 1)],
        3: [(add_side, 3)],
        4: [(forward, 1), (add_line, 2)],
        5: [],
        6: [(forward, 2), (add_line, 3)],
        7: [],
    }

    def step(kk, carry):
        here = pl.ds(pl.multiple_of(kk * BLOCK, BLOCK), BLOCK)
        factor = factor_block(work[here, here])
        pivot_rows = jnp.dot(factor, work[here, :], precision=HIGHEST, preferred_element_type=F32)
        wide = jnp.concatenate([factor] * blocks, axis=1)
        pivot_rows = jnp.where(column_block == kk, wide, pivot_rows)
        work[here, :] = pivot_rows

        def below(i, carry):
            there = pl.ds(pl.multiple_of(i * BLOCK, BLOCK), BLOCK)
            panel = lax.dot_general(
                work[there, here], factor, (((1,), (1,)), ((), ())),
                precision=HIGHEST, preferred_element_type=F32,
            )
            work[there, here] = jnp.zeros((BLOCK, BLOCK), F32)
            work[there, :] = work[there, :] - jnp.dot(
                panel, work[here, :], precision=HIGHEST, preferred_element_type=F32
            )
            return carry

        lax.fori_loop(kk + 1, blocks, below, 0)
        rest = jnp.where(column_block <= kk, pivot_rows, 0.0)
        high = rest.astype(BF16)
        inverse[0, here, :] = high
        inverse[1, here, :] = (rest - high.astype(F32)).astype(BF16)
        for at, todo in events.items():
            if todo:
                @pl.when(kk == at)
                def _(todo=todo):
                    for function, j in todo:
                        function(j)
        return carry

    lax.fori_loop(0, blocks, step, 0)
    forward(3)

    def apply(load_right, store_out, columns):
        tile = 512

        def one(n, carry):
            here = pl.ds(pl.multiple_of(n * tile, tile), tile)
            right = load_right(here)
            for i in range(4):
                rows = slice(256 * i, 256 * (i + 1))
                deep = 256 * (i + 1)
                left = inverse[:, rows, :deep].reshape(512, deep)
                value = jnp.dot(left, right[:deep], preferred_element_type=F32)
                store_out(i, here, value[:256] + value[256:])
            return carry

        lax.fori_loop(0, columns // tile, one, 0)

    def p_load(here):
        return pt_ref[:, :, :, here].reshape(rank, 512)

    def o_store(i, here, value):
        ot_ref[256 * i : 256 * (i + 1), here] = value.astype(BF16)

    apply(p_load, o_store, pt_ref.shape[3])
    squares[...] = jnp.zeros_like(squares)

    def store(j):
        return pltpu.make_async_copy(
            wpart.at[j], n_hbm.at[:, :, :, pl.ds(j * width, width)], store_sem.at[j]
        )

    for j in range(chunks):
        for shift in range(4):
            full_side_in(j, shift).wait_recv()
        side_out(j).wait_send()

        def w_load(here, j=j):
            return whole[j, :, :, :, here].reshape(rank, 512)

        def n_store(i, here, value, j=j):
            low = value.astype(BF16)
            wpart[j, i, :, :, here] = low.reshape(2, ranks, 512)
            low = low.astype(F32)
            low = low * low
            squares[256 * i : 256 * (i + 1), :] += sum(
                low[:, BLOCK * g : BLOCK * (g + 1)] for g in range(1, 4)
            ) + low[:, :BLOCK]

        apply(w_load, n_store, width)
        store(j).start()

    def norm(shift):
        to = lax.rem(col + shift, 4)
        return remote(norm_in.at[col], norm_in.at[col], ns.at[shift], nr.at[col], (row, to))

    def norm_from(shift):
        who = lax.rem(col + shift, 4)
        return remote(norm_in.at[who], norm_in.at[who], ns.at[shift], nr.at[who], (row, who))

    ones = jnp.ones((GROUP, BLOCK), F32)
    norm_in[col] = lax.dot_general(
        ones, squares[...], (((1,), (1,)), ((), ())), precision=HIGHEST, preferred_element_type=F32
    )
    for shift in range(1, 4):
        norm(shift).start()
    for shift in range(1, 4):
        norm_from(shift).wait_recv()
    sums_ref[...] = (norm_in[0] + norm_in[1]) + (norm_in[2] + norm_in[3])
    for shift in range(1, 4):
        norm(shift).wait_send()
    for shift in range(1, 8):
        gram_out(shift).wait_send()
        sum_out(shift).wait_send()
    spread(0, col, core_peer).wait_send()
    spread(1, col, y_peer).wait_send()
    spread(2, other_col, core_peer).wait_send()
    for j in range(chunks):
        for shift in (1, 2, 3):
            line_out(j, shift).wait_send()
            full_out(j, shift).wait_send()
        for shift in range(4):
            full_side(j, shift).wait_send()
        store(j).wait()


def factorize(pt, b):
    _, _, ranks, rows = pt.shape
    columns = b.shape[1]
    rank = 8 * ranks
    width = columns // CHUNKS
    slice_rows = STACK * BLOCK // 8
    dma = pltpu.SemaphoreType.DMA
    vmem = pl.BlockSpec(memory_space=pltpu.VMEM)
    anywhere = pl.BlockSpec(memory_space=pl.ANY)
    return pl.pallas_call(
        factor_kernel,
        out_shape=(
            jax.ShapeDtypeStruct((rank, rows), BF16),
            jax.ShapeDtypeStruct((4, 2, ranks, columns), BF16),
            jax.ShapeDtypeStruct((GROUP, rank), F32),
        ),
        in_specs=[vmem, anywhere],
        out_specs=(vmem, anywhere, vmem),
        scratch_shapes=[
            pltpu.VMEM((2, rows, width), BF16),
            pltpu.VMEM((CHUNKS, 4, 2, ranks, width), BF16),
            pltpu.VMEM((CHUNKS, 4, ranks, width), BF16),
            pltpu.VMEM((CHUNKS, 4, ranks, width), BF16),
            pltpu.VMEM((CHUNKS, 4, 2, ranks, width), BF16),
            pltpu.VMEM((STACK * BLOCK, BLOCK), F32),
            pltpu.VMEM((8, slice_rows, BLOCK), F32),
            pltpu.VMEM((4, STACK * BLOCK, BLOCK), F32),
            pltpu.VMEM((rank, rank), F32),
            pltpu.VMEM((2, rank, rank), BF16),
            pltpu.VMEM((rank, BLOCK), F32),
            pltpu.VMEM((4, GROUP, rank), F32),
            dma((2,)), dma((CHUNKS,)), dma((CHUNKS,)), dma((CHUNKS,)),
            dma((CHUNKS, 4)), dma((CHUNKS, 4)), dma((CHUNKS, 4)), dma((CHUNKS, 4)),
            dma((CHUNKS, 4)), dma((CHUNKS, 4)), dma((1,)),
            dma((8,)), dma((8,)), dma((8,)), dma((8,)), dma((3,)), dma((3,)), dma((4,)), dma((4,)),
        ],
        compiler_params=pltpu.CompilerParams(
            collective_id=2, has_side_effects=True, vmem_limit_bytes=58 * 1024 * 1024
        ),
        name="factorize",
    )(pt, b)


def body(momentum, gradient, right_basis):
    pt, buffer = project(right_basis, momentum, gradient)
    ortho, right_new, sums = factorize(pt, buffer)
    rank = ortho.shape[0]
    rank_rows = right_basis.shape[0]
    right_new = right_new.reshape(rank, buffer.shape[1])
    inverse_norm = lax.rsqrt(sums[0] + epsilon)
    first = lax.axis_index("row") * rank_rows
    mine = lax.dynamic_slice_in_dim(right_new, first, rank_rows, axis=0)
    mine_norm = lax.dynamic_slice_in_dim(inverse_norm, first, rank_rows, axis=0)
    basis_next = mine.astype(F32) * mine_norm[:, None]
    scaled = (right_new.astype(F32) * inverse_norm[:, None]).astype(BF16)
    dims = (((0,), (0,)), ((), ()))
    feedback = lax.dot_general(ortho, right_new, dims, preferred_element_type=F32)
    direction = lax.dot_general(ortho, scaled, dims, preferred_element_type=F32)
    momentum_next = (buffer.astype(F32) - (1.0 - momentum_decay) * feedback).astype(BF16)
    update = (D / math.sqrt(RANK) * direction).astype(BF16)
    return (momentum_next, basis_next, update)


def solution(mesh):
    sizes = (mesh.shape["row"], mesh.shape["col"])
    return jax.shard_map(
        body if sizes == (8, 4) else plain_body,
        mesh=mesh,
        in_specs=(P("row", "col"), P("row", "col"), P("row", "col")),
        out_specs=(P("row", "col"), P("row", "col"), P("row", "col")),
        check_vma=False,
    )
```

```python
import functools
import math

import jax
import jax.numpy as jnp
from jax import lax
from jax.experimental import pallas as pl
from jax.experimental.pallas import tpu as pltpu
from jax.sharding import PartitionSpec as P

D = 16384
RANK = 1024

momentum_decay = 0.95
epsilon = 1e-06

BLOCK = 128
GROUP = 8
PACK = 256

HIGHEST = lax.Precision.HIGHEST


def across(x, column):
    return jnp.broadcast_to(x[:, column : column + 1], (x.shape[0], BLOCK))


def down(x, row):
    return jnp.broadcast_to(x[row : row + 1, :], (GROUP, BLOCK))


def factor_block(block):
    groups = BLOCK // GROUP
    sub = lax.broadcasted_iota(jnp.int32, (GROUP, BLOCK), 0)
    lane = lax.broadcasted_iota(jnp.int32, (GROUP, BLOCK), 1)
    left = [block[GROUP * g : GROUP * (g + 1), :] for g in range(groups)]
    right = [jnp.where(lane == sub + GROUP * g, 1.0, 0.0) for g in range(groups)]
    inverse = []
    for g in range(groups):
        first = GROUP * g
        jordan_left, jordan_right = left[g], right[g]
        columns = [across(jordan_left, first + l) for l in range(GROUP)]
        forward_right, pivots = jordan_right, jnp.ones_like(jordan_left)
        for l in range(GROUP):
            pivot = down(columns[l], l)
            reciprocal = 1.0 / pivot
            mine = sub == l
            column = columns[l]
            row_left, row_right = down(jordan_left, l), down(jordan_right, l)
            forward_right = jnp.where(mine, row_right, forward_right)
            pivots = jnp.where(mine, pivot, pivots)
            row_left, row_right = row_left * reciprocal, row_right * reciprocal
            jordan_left = jnp.where(mine, row_left, jordan_left - column * row_left)
            jordan_right = jnp.where(mine, row_right, jordan_right - column * row_right)
            for m in range(l + 1, GROUP):
                row = down(columns[m], l) * reciprocal
                columns[m] = jnp.where(mine, row, columns[m] - column * row)
        inverse.append(forward_right * lax.rsqrt(pivots))
        rows_left = [down(jordan_left, l) for l in range(GROUP)]
        rows_right = [down(jordan_right, l) for l in range(GROUP)]
        for h in range(g + 1, groups):
            base = left[h]
            new_left, new_right = base, right[h]
            for l in range(GROUP):
                coefficient = across(base, first + l)
                new_left = new_left - coefficient * rows_left[l]
                new_right = new_right - coefficient * rows_right[l]
            left[h], right[h] = new_left, new_right
    return jnp.concatenate(inverse, axis=0)


def plain_factor_kernel(packed_ref, share_ref, ortho_ref, work):
    rank = work.shape[0]
    blocks = rank // BLOCK
    offset = 0
    for i in range(rank // PACK):
        for j in range(i + 1):
            tile = packed_ref[:, offset : offset + PACK]
            offset += PACK
            work[PACK * i : PACK * (i + 1), PACK * j : PACK * (j + 1)] = tile
            if j < i:
                work[PACK * j : PACK * (j + 1), PACK * i : PACK * (i + 1)] = tile.T
    column_block = lax.broadcasted_iota(jnp.int32, (BLOCK, rank), 1) // BLOCK

    def step(k, carry):
        here = pl.ds(pl.multiple_of(k * BLOCK, BLOCK), BLOCK)
        x = factor_block(work[here, here])
        pivot_rows = jnp.dot(x, work[here, :], precision=HIGHEST, preferred_element_type=jnp.float32)
        wide = jnp.concatenate([x] * blocks, axis=1)
        pivot_rows = jnp.where(column_block == k, wide, pivot_rows)
        work[here, :] = pivot_rows

        def below(i, carry):
            there = pl.ds(pl.multiple_of(i * BLOCK, BLOCK), BLOCK)
            panel = lax.dot_general(
                work[there, here], x, (((1,), (1,)), ((), ())),
                precision=HIGHEST, preferred_element_type=jnp.float32,
            )
            work[there, here] = jnp.zeros((BLOCK, BLOCK), jnp.float32)
            work[there, :] = work[there, :] - jnp.dot(
                panel, work[here, :], precision=HIGHEST, preferred_element_type=jnp.float32
            )
            return carry

        lax.fori_loop(k + 1, blocks, below, 0)
        rest = jnp.where(column_block <= k, pivot_rows, 0.0)
        total = jnp.zeros((share_ref.shape[0], BLOCK), jnp.float32)
        for _ in range(3):
            part = rest.astype(jnp.bfloat16)
            rest = rest - part.astype(jnp.float32)
            total = total + lax.dot_general(
                share_ref[...], part, (((1,), (1,)), ((), ())),
                preferred_element_type=jnp.float32,
            )
        ortho_ref[:, here] = total.astype(jnp.bfloat16)
        return carry

    lax.fori_loop(0, blocks, step, 0)


def orthonormalize(row_share, packed):
    rank = row_share.shape[1]
    return pl.pallas_call(
        plain_factor_kernel,
        out_shape=jax.ShapeDtypeStruct(row_share.shape, jnp.bfloat16),
        in_specs=[pl.BlockSpec(memory_space=pltpu.VMEM)] * 2,
        out_specs=pl.BlockSpec(memory_space=pltpu.VMEM),
        scratch_shapes=[pltpu.VMEM((rank, rank), jnp.float32)],
        compiler_params=pltpu.CompilerParams(vmem_limit_bytes=40 * 1024 * 1024),
        name="factor",
    )(packed, row_share)


def packed_gram(share):
    pieces = []
    for i in range(share.shape[1] // PACK):
        pieces.append(
            lax.dot_general(
                share[:, PACK * i : PACK * (i + 1)],
                share[:, : PACK * (i + 1)],
                (((0,), (0,)), ((), ())),
                preferred_element_type=jnp.float32,
            )
        )
    return jnp.concatenate(pieces, axis=1)


def plain_body(momentum, gradient, right_basis):
    buffer = (momentum.astype(jnp.float32) + gradient.astype(jnp.float32)).astype(jnp.bfloat16)
    rank_rows = right_basis.shape[0]
    partial_value = lax.dot_general(
        buffer,
        lax.all_gather(right_basis, "row", axis=0, tiled=True),
        (((1,), (1,)), ((), ())),
        preferred_element_type=jnp.float32,
    )
    row_share = lax.psum_scatter(
        partial_value.astype(jnp.bfloat16), "col", scatter_dimension=0, tiled=True
    )
    packed = lax.psum(packed_gram(row_share), ("row", "col"))
    ortho_share = orthonormalize(row_share, packed)
    orthonormal = lax.all_gather(ortho_share, "col", axis=0, tiled=True)
    right_share = lax.psum_scatter(
        lax.dot_general(
            orthonormal, buffer, (((0,), (0,)), ((), ())), preferred_element_type=jnp.float32
        ).astype(jnp.bfloat16),
        "row",
        scatter_dimension=0,
        tiled=True,
    )
    gathered = lax.all_gather(right_share, "row", axis=0, tiled=True)
    right_wide = right_share.astype(jnp.float32)
    sums = jnp.sum(right_wide * right_wide, axis=1)
    everyone = lax.all_gather(sums, ("row", "col"), axis=0)
    everyone = everyone.reshape(lax.axis_size("row"), lax.axis_size("col"), rank_rows)
    inverse_rows = lax.rsqrt(jnp.sum(everyone, axis=1) + epsilon)
    inverse_norm = inverse_rows.reshape(-1, 1)
    mine = lax.dynamic_index_in_dim(inverse_rows, lax.axis_index("row"), 0, keepdims=False)
    basis_next = right_wide * mine[:, None]
    scaled = (gathered.astype(jnp.float32) * inverse_norm).astype(jnp.bfloat16)
    feedback = jnp.dot(orthonormal, gathered, preferred_element_type=jnp.float32)
    direction = jnp.dot(orthonormal, scaled, preferred_element_type=jnp.float32)
    momentum_next = (buffer.astype(jnp.float32) - (1.0 - momentum_decay) * feedback).astype(
        jnp.bfloat16
    )
    update_scale = D / math.sqrt(RANK)
    update = (update_scale * direction).astype(jnp.bfloat16)
    return (momentum_next, basis_next, update)


MESH = pl.DeviceIdType.MESH
CHUNKS = 4
STACK = 9
F32 = jnp.float32
BF16 = jnp.bfloat16


def remote(src, dst, send_sem, recv_sem, device):
    return pltpu.make_async_remote_copy(
        src_ref=src, dst_ref=dst, send_sem=send_sem, recv_sem=recv_sem,
        device_id=device, device_id_type=MESH,
    )


def places():
    row, col = lax.axis_index("row"), lax.axis_index("col")
    return row, col, row // 2, lax.rem(row, 2), col // 2, lax.rem(col, 2)


def greet(devices):
    barrier = pltpu.get_barrier_semaphore()
    for device in devices:
        pl.semaphore_signal(barrier, inc=1, device_id=device, device_id_type=MESH)
    pl.semaphore_wait(barrier, len(devices))


def nt_dot(a, b):
    return lax.dot_general(a, b, (((1,), (1,)), ((), ())), preferred_element_type=F32)


def project_kernel(
    v_ref, m_hbm, g_hbm, pt_ref, b_hbm,
    buf, basis, m_tile, g_tile, part, core_in, half, y_in,
    load_sem, store_sem, own_send, hop_send, x_send, z_recv, x_recv,
    core_send, core_recv, y_send, y_recv, share_send, share_recv,
):
    row, col, z, x, y, k = places()
    rows = buf.shape[0]
    tile = m_tile.shape[1]
    tiles = rows // tile
    x_peer = (z * 2 + 1 - x, col)
    core_peer = (row, y * 2 + 1 - k)
    y_peer = (row, (1 - y) * 2 + k)
    middle = jnp.logical_and(z > 0, z < 3)
    order = [z, jnp.bitwise_xor(z, 1), jnp.where(z < 2, 2, 1), jnp.where(z < 2, 3, 0)]

    def load(i, slot):
        here = pl.ds(pl.multiple_of(i * tile, tile), tile)
        return (
            pltpu.make_async_copy(m_hbm.at[here], m_tile.at[slot], load_sem.at[0, slot]),
            pltpu.make_async_copy(g_hbm.at[here], g_tile.at[slot], load_sem.at[1, slot]),
        )

    for slot in range(2):
        for copy in load(slot, slot):
            copy.start()
    greet(
        [(lax.rem(z + 1, 4) * 2 + x, col), (lax.rem(z + 2, 4) * 2 + x, col), (lax.rem(z + 3, 4) * 2 + x, col)]
        + [x_peer, core_peer, y_peer]
    )
    own_up = remote(v_ref, basis.at[z, x], own_send.at[0], z_recv.at[z], (jnp.minimum(z + 1, 3) * 2 + x, col))
    own_down = remote(v_ref, basis.at[z, x], own_send.at[1], z_recv.at[z], (jnp.maximum(z - 1, 0) * 2 + x, col))
    own_side = remote(v_ref, basis.at[z, x], x_send.at[z], x_recv.at[z], x_peer)

    @pl.when(z < 3)
    def _():
        own_up.start()

    @pl.when(z > 0)
    def _():
        own_down.start()

    own_side.start()
    basis[z, x] = v_ref[...]

    def build(i, carry):
        slot = lax.rem(i, 2)
        for copy in load(i, slot):
            copy.wait()
        here = pl.ds(pl.multiple_of(i * tile, tile), tile)
        buf[here, :] = (m_tile[slot].astype(F32) + g_tile[slot].astype(F32)).astype(BF16)

        @pl.when(i + 2 < tiles)
        def _():
            for copy in load(i + 2, slot):
                copy.start()

        return carry

    lax.fori_loop(0, tiles, build, 0)
    store = pltpu.make_async_copy(buf, b_hbm, store_sem)
    store.start()

    def hop(s):
        q = order[s]
        target = jnp.where(z == 1, jnp.where(q < z, 2, 0), jnp.where(q < z, 3, 1))
        return remote(basis.at[q, x], basis.at[q, x], hop_send.at[s - 1], z_recv.at[q], (target * 2 + x, col))

    def side(s):
        q = order[s]
        return remote(basis.at[q, x], basis.at[q, x], x_send.at[q], x_recv.at[q], x_peer)

    def take(s):
        hop(s).wait_recv()

        @pl.when(middle)
        def _():
            hop(s).start()

        side(s).start()

    def side_in(s):
        q = order[s]
        remote(basis.at[q, x], basis.at[q, 1 - x], x_send.at[q], x_recv.at[q], x_peer).wait_recv()

    def to_core(s):
        return remote(part.at[s, 1 - k], core_in.at[s], core_send.at[s], core_recv.at[s], core_peer)

    def to_y(s):
        return remote(half.at[s], y_in.at[s], y_send.at[s], y_recv.at[s], y_peer)

    def share(s):
        return remote(pt_ref.at[order[s], k], pt_ref.at[order[s], k], share_send.at[s], share_recv.at[s], core_peer)

    def share_in(s):
        return remote(pt_ref.at[order[s], k], pt_ref.at[order[s], 1 - k], share_send.at[s], share_recv.at[s], core_peer)

    def multiply(s):
        q = order[s]
        width = 512

        def columns(n, carry):
            here = pl.ds(pl.multiple_of(n * width, width), width)
            left = basis[q].reshape(2 * basis.shape[2], basis.shape[3])
            value = nt_dot(left, buf[here, :])
            part[s, :, :, here] = value.astype(BF16).reshape(2, basis.shape[2], width)
            return carry

        lax.fori_loop(0, rows // width, columns, 0)
        to_core(s).start()

    def add_core(s):
        to_core(s).wait_recv()
        half[s] = (part[s, k].astype(F32) + core_in[s].astype(F32)).astype(BF16)
        to_y(s).start()

    def add_y(s):
        to_y(s).wait_recv()
        pt_ref[order[s], k] = (half[s].astype(F32) + y_in[s].astype(F32)).astype(BF16)
        share(s).start()

    take(1)

    @pl.when(middle)
    def _():
        take(2)

    side_in(0)
    multiply(0)

    @pl.when(jnp.logical_not(middle))
    def _():
        take(2)

    add_core(0)

    @pl.when(middle)
    def _():
        take(3)

    side_in(1)
    multiply(1)
    add_y(0)
    add_core(1)

    @pl.when(jnp.logical_not(middle))
    def _():
        take(3)

    side_in(2)
    multiply(2)
    add_y(1)
    add_core(2)
    side_in(3)
    multiply(3)
    add_y(2)
    add_core(3)
    add_y(3)

    @pl.when(z < 3)
    def _():
        own_up.wait_send()

    @pl.when(z > 0)
    def _():
        own_down.wait_send()

    own_side.wait_send()

    @pl.when(middle)
    def _():
        for s in range(1, 4):
            hop(s).wait_send()

    for s in range(1, 4):
        side(s).wait_send()
    for s in range(4):
        to_core(s).wait_send()
        to_y(s).wait_send()
        share(s).wait_send()
        share_in(s).wait_recv()
    store.wait()


def project(v, m, g):
    rows, columns = m.shape
    ranks = v.shape[0]
    dma = pltpu.SemaphoreType.DMA
    vmem = pl.BlockSpec(memory_space=pltpu.VMEM)
    anywhere = pl.BlockSpec(memory_space=pl.ANY)
    return pl.pallas_call(
        project_kernel,
        out_shape=(
            jax.ShapeDtypeStruct((4, 2, ranks, rows), BF16),
            jax.ShapeDtypeStruct((rows, columns), BF16),
        ),
        in_specs=[vmem, anywhere, anywhere],
        out_specs=(vmem, anywhere),
        scratch_shapes=[
            pltpu.VMEM((rows, columns), BF16),
            pltpu.VMEM((4, 2, ranks, columns), BF16),
            pltpu.VMEM((2, 128, columns), BF16),
            pltpu.VMEM((2, 128, columns), BF16),
            pltpu.VMEM((4, 2, ranks, rows), BF16),
            pltpu.VMEM((4, ranks, rows), BF16),
            pltpu.VMEM((4, ranks, rows), BF16),
            pltpu.VMEM((4, ranks, rows), BF16),
            dma((2, 2)), dma, dma((2,)), dma((3,)), dma((4,)), dma((4,)), dma((4,)),
            dma((4,)), dma((4,)), dma((4,)), dma((4,)), dma((4,)), dma((4,)),
        ],
        compiler_params=pltpu.CompilerParams(
            collective_id=1, has_side_effects=True, vmem_limit_bytes=58 * 1024 * 1024
        ),
        cost_estimate=pl.CostEstimate(flops=2 * rows * columns * ranks * 8, bytes_accessed=6 * rows * columns, transcendentals=0),
        name="project",
    )(v, m, g)


def factor_kernel(
    pt_ref, b_hbm, ot_ref, n_hbm, sums_ref,
    buf, wpart, x_in, z_in, whole, stack, stack_in, stack_all, work, inverse, squares, norm_in,
    load_sem, store_sem, xs, xr, zs, zr, gs, gr, fs, ys,
    ss, sr, ts, tr, us, ur, ns, nr,
):
    row, col, z, x, y, k = places()
    ranks = pt_ref.shape[2]
    rank = work.shape[0]
    blocks = rank // BLOCK
    chunks = wpart.shape[0]
    width = wpart.shape[4]
    slice_rows = stack_in.shape[1]
    x_peer = (z * 2 + 1 - x, col)
    core_peer = (row, y * 2 + 1 - k)
    y_peer = (row, (1 - y) * 2 + k)

    def z_of(shift):
        return lax.rem(z + shift, 4)

    def z_peer(shift):
        return (z_of(shift) * 2 + x, col)

    def row_of(shift):
        return lax.rem(row + shift, 8)

    def load(j):
        return pltpu.make_async_copy(
            b_hbm.at[:, pl.ds(j * width, width)], buf.at[j % 2], load_sem.at[j % 2]
        )

    load(0).start()
    load(1).start()
    greet([(row_of(shift), col) for shift in range(1, 8)] + [core_peer, y_peer])

    def gram(t, carry):
        early = t < 8 - col
        i = jnp.where(early, col + t, t - 1)
        j = jnp.where(early, col, 7 - col)
        value = nt_dot(pt_ref[i // 2, lax.rem(i, 2)], pt_ref[j // 2, lax.rem(j, 2)])
        stack[pl.ds(pl.multiple_of(t * BLOCK, BLOCK), BLOCK), :] = value
        return carry

    lax.fori_loop(0, STACK, gram, 0)

    def part_of(r):
        return pl.ds(pl.multiple_of(r * slice_rows, slice_rows), slice_rows)

    def gram_out(shift):
        to = row_of(shift)
        return remote(stack.at[part_of(to)], stack_in.at[row], ss.at[shift], sr.at[row], (to, col))

    def gram_in(shift):
        who = row_of(shift)
        return remote(stack.at[part_of(row)], stack_in.at[who], ss.at[shift], sr.at[who], (who, col))

    def sum_out(shift):
        to = row_of(shift)
        return remote(stack_all.at[col, part_of(row)], stack_all.at[col, part_of(row)], ts.at[shift], tr.at[row], (to, col))

    def sum_in(shift):
        who = row_of(shift)
        return remote(stack_all.at[col, part_of(who)], stack_all.at[col, part_of(who)], ts.at[shift], tr.at[who], (who, col))

    def spread(index, what, device):
        return remote(stack_all.at[what], stack_all.at[what], us.at[index], ur.at[index], device)

    for shift in range(1, 8):
        gram_out(shift).start()

    def side_out(j):
        return remote(wpart.at[j, :, 1 - x], x_in.at[j], xs.at[j], xr.at[j], x_peer)

    def weigh(j, which):
        step = 256

        def columns(n, carry):
            here = pl.ds(pl.multiple_of(n * step, step), step)
            left = pt_ref[:, which].reshape(4 * ranks, pt_ref.shape[3])
            value = jnp.dot(left, buf[j % 2, :, here], preferred_element_type=F32)
            wpart[j, :, which, :, here] = value.astype(BF16).reshape(4, ranks, step)
            return carry

        lax.fori_loop(0, width // step, columns, 0)

    def product(j):
        load(j).wait()
        weigh(j, 1 - x)
        side_out(j).start()
        weigh(j, x)
        if j + 2 < chunks:
            load(j + 2).start()

    end = jnp.logical_or(z == 0, z == 3)
    low = z < 2

    def line_send(j, i, piece, to, slot):
        return remote(x_in.at[j, piece], z_in.at[j, slot], zs.at[j, i], zr.at[j, slot], (to * 2 + x, col))

    def line_take(j, slot):
        remote(x_in.at[j, 0], z_in.at[j, slot], zs.at[j, 0], zr.at[j, slot], x_peer).wait_recv()

    def line_first(j):
        for i in range(3):
            piece = jnp.where(low, 3 - i, i)
            slot = piece if i < 2 else jnp.where(low, 1, 4)
            line_send(j, i, piece, jnp.where(low, 1, 2), slot).start()

    def add_in(j, piece):
        line_take(j, piece)
        x_in[j, piece] = (x_in[j, piece].astype(F32) + z_in[j, piece].astype(F32)).astype(BF16)

    def add_side(j):
        side_out(j).wait_recv()
        for shift in (1, 2, 3, 0):
            there = z_of(shift)
            x_in[j, there] = (wpart[j, there, x].astype(F32) + x_in[j, there].astype(F32)).astype(BF16)

        @pl.when(end)
        def _():
            line_first(j)

    def line_second(j):
        @pl.when(jnp.logical_not(end))
        def _():
            for i in range(2):
                piece = jnp.where(low, 3 - i, i)
                slot = piece if i < 1 else jnp.where(low, 2, 4)
                add_in(j, piece)
                line_send(j, i, piece, jnp.where(low, 2, 1), slot).start()

    def line_third(j):
        @pl.when(jnp.logical_not(end))
        def _():
            piece = jnp.where(low, 0, 3)
            add_in(j, piece)
            line_send(j, 2, piece, piece, jnp.where(low, 4, 3)).start()

    order = [z, jnp.bitwise_xor(z, 1), jnp.where(low, 2, 1), jnp.where(low, 3, 0)]

    def full_send(j, q, sem, to):
        return remote(whole.at[j, q, x], whole.at[j, q, x], gs.at[j, sem], gr.at[j, q], (to * 2 + x, col))

    def own_up(j):
        return full_send(j, z, 0, jnp.minimum(z + 1, 3))

    def own_down(j):
        return full_send(j, z, 1, jnp.maximum(z - 1, 0))

    def hop(j, s):
        q = order[s]
        return full_send(j, q, s + 1, jnp.where(low, jnp.where(q < z, 2, 0), jnp.where(q < z, 3, 1)))

    def full_side(j, q):
        return remote(whole.at[j, q, x], whole.at[j, q, x], fs.at[j, q], ys.at[j, q], x_peer)

    def full_side_in(j, q):
        return remote(whole.at[j, q, x], whole.at[j, q, 1 - x], fs.at[j, q], ys.at[j, q], x_peer)

    def finish(j):
        @pl.when(z > 0)
        def _():
            line_take(j, z)
            x_in[j, z] = (x_in[j, z].astype(F32) + z_in[j, z].astype(F32)).astype(BF16)

        @pl.when(z < 3)
        def _():
            line_take(j, 4)
            x_in[j, z] = (x_in[j, z].astype(F32) + z_in[j, 4].astype(F32)).astype(BF16)

        whole[j, z, x] = x_in[j, z]

        @pl.when(z < 3)
        def _():
            own_up(j).start()

        @pl.when(z > 0)
        def _():
            own_down(j).start()

        full_side(j, z).start()

    def take(j, s):
        hop(j, s).wait_recv()

        @pl.when(jnp.logical_not(end))
        def _():
            hop(j, s).start()

        full_side(j, order[s]).start()

    def take_first(j):
        take(j, 1)

        @pl.when(jnp.logical_not(end))
        def _():
            take(j, 2)

    def take_second(j):
        @pl.when(end)
        def _():
            take(j, 2)

    def take_third(j):
        take(j, 3)

    def sum_gram():
        total = stack[part_of(row), :]
        for shift in range(1, 8):
            gram_in(shift).wait_recv()
            total = total + stack_in[row_of(shift)]
        stack_all[col, part_of(row), :] = total
        for shift in range(1, 8):
            sum_out(shift).start()

    other_col = (1 - y) * 2 + k

    def spread_gram():
        for shift in range(1, 8):
            sum_in(shift).wait_recv()
        spread(1, col, y_peer).start()
        spread(0, col, core_peer).start()

    def end_gram():
        spread(1, other_col, y_peer).wait_recv()
        spread(2, other_col, core_peer).start()
        spread(0, y * 2 + 1 - k, core_peer).wait_recv()
        spread(2, (1 - y) * 2 + 1 - k, core_peer).wait_recv()

    product(0)
    product(1)
    add_side(0)
    product(2)
    product(3)
    line_second(0)
    sum_gram()
    add_side(1)
    line_third(0)
    finish(0)
    spread_gram()
    line_second(1)
    line_third(1)
    add_side(2)
    take_first(0)
    finish(1)
    end_gram()
    line_second(2)

    for c in range(4):
        for t in range(STACK):
            i, j = (c + t, c) if t < 8 - c else (t - 1, 7 - c)
            value = stack_all[c, BLOCK * t : BLOCK * (t + 1), :]
            work[BLOCK * i : BLOCK * (i + 1), BLOCK * j : BLOCK * (j + 1)] = value
            if i != j:
                work[BLOCK * j : BLOCK * (j + 1), BLOCK * i : BLOCK * (i + 1)] = value.T

    column_block = lax.broadcasted_iota(jnp.int32, (BLOCK, rank), 1) // BLOCK
    events = {
        0: [(add_side, 3), (line_third, 2)],
        1: [(take_first, 1), (finish, 2)],
        2: [(line_second, 3)],
        3: [(take_second, 1), (take_first, 2), (line_third, 3), (take_second, 0), (take_second, 2)],
        4: [(finish, 3)],
        5: [(take_third, 0)],
        6: [(take_third, 1), (take_third, 2), (take_first, 3)],
        7: [],
    }

    def step(kk, carry):
        here = pl.ds(pl.multiple_of(kk * BLOCK, BLOCK), BLOCK)
        factor = factor_block(work[here, here])
        pivot_rows = jnp.dot(factor, work[here, :], precision=HIGHEST, preferred_element_type=F32)
        wide = jnp.concatenate([factor] * blocks, axis=1)
        pivot_rows = jnp.where(column_block == kk, wide, pivot_rows)
        work[here, :] = pivot_rows

        def below(i, carry):
            there = pl.ds(pl.multiple_of(i * BLOCK, BLOCK), BLOCK)
            panel = lax.dot_general(
                work[there, here], factor, (((1,), (1,)), ((), ())),
                precision=HIGHEST, preferred_element_type=F32,
            )
            work[there, here] = jnp.zeros((BLOCK, BLOCK), F32)
            work[there, :] = work[there, :] - jnp.dot(
                panel, work[here, :], precision=HIGHEST, preferred_element_type=F32
            )
            return carry

        lax.fori_loop(kk + 1, blocks, below, 0)
        rest = jnp.where(column_block <= kk, pivot_rows, 0.0)
        high = rest.astype(BF16)
        inverse[0, here, :] = high
        inverse[1, here, :] = (rest - high.astype(F32)).astype(BF16)
        for at, todo in events.items():
            if todo:
                @pl.when(kk == at)
                def _(todo=todo):
                    for function, j in todo:
                        function(j)
        return carry

    lax.fori_loop(0, blocks, step, 0)

    def apply(load_right, store_out, columns):
        tile = 512

        def one(n, carry):
            here = pl.ds(pl.multiple_of(n * tile, tile), tile)
            right = load_right(here)
            for i in range(4):
                rows = slice(256 * i, 256 * (i + 1))
                deep = 256 * (i + 1)
                left = inverse[:, rows, :deep].reshape(512, deep)
                value = jnp.dot(left, right[:deep], preferred_element_type=F32)
                store_out(i, here, value[:256] + value[256:])
            return carry

        lax.fori_loop(0, columns // tile, one, 0)

    def p_load(here):
        return pt_ref[:, :, :, here].reshape(rank, 512)

    def o_store(i, here, value):
        ot_ref[256 * i : 256 * (i + 1), here] = value.astype(BF16)

    apply(p_load, o_store, pt_ref.shape[3])
    take_second(3)
    take_third(3)
    squares[...] = jnp.zeros_like(squares)

    def store(j):
        return pltpu.make_async_copy(
            wpart.at[j], n_hbm.at[:, :, :, pl.ds(j * width, width)], store_sem.at[j]
        )

    for j in range(chunks):
        for q in range(4):
            full_side_in(j, q).wait_recv()
        side_out(j).wait_send()

        def w_load(here, j=j):
            return whole[j, :, :, :, here].reshape(rank, 512)

        def n_store(i, here, value, j=j):
            low = value.astype(BF16)
            wpart[j, i, :, :, here] = low.reshape(2, ranks, 512)
            low = low.astype(F32)
            low = low * low
            squares[256 * i : 256 * (i + 1), :] += sum(
                low[:, BLOCK * g : BLOCK * (g + 1)] for g in range(1, 4)
            ) + low[:, :BLOCK]

        apply(w_load, n_store, width)
        store(j).start()

    def norm(shift):
        to = lax.rem(col + shift, 4)
        return remote(norm_in.at[col], norm_in.at[col], ns.at[shift], nr.at[col], (row, to))

    def norm_from(shift):
        who = lax.rem(col + shift, 4)
        return remote(norm_in.at[who], norm_in.at[who], ns.at[shift], nr.at[who], (row, who))

    ones = jnp.ones((GROUP, BLOCK), F32)
    norm_in[col] = lax.dot_general(
        ones, squares[...], (((1,), (1,)), ((), ())), precision=HIGHEST, preferred_element_type=F32
    )
    for shift in range(1, 4):
        norm(shift).start()
    for shift in range(1, 4):
        norm_from(shift).wait_recv()
    sums_ref[...] = (norm_in[0] + norm_in[1]) + (norm_in[2] + norm_in[3])
    for shift in range(1, 4):
        norm(shift).wait_send()
    for shift in range(1, 8):
        gram_out(shift).wait_send()
        sum_out(shift).wait_send()
    spread(0, col, core_peer).wait_send()
    spread(1, col, y_peer).wait_send()
    spread(2, other_col, core_peer).wait_send()
    for j in range(chunks):
        for i in range(3):
            line_send(j, i, 0, z, 0).wait_send()

        @pl.when(z < 3)
        def _():
            own_up(j).wait_send()

        @pl.when(z > 0)
        def _():
            own_down(j).wait_send()

        @pl.when(jnp.logical_not(end))
        def _():
            for s in range(1, 4):
                hop(j, s).wait_send()

        for q in range(4):
            full_side(j, q).wait_send()
        store(j).wait()


def factorize(pt, b):
    _, _, ranks, rows = pt.shape
    columns = b.shape[1]
    rank = 8 * ranks
    width = columns // CHUNKS
    slice_rows = STACK * BLOCK // 8
    dma = pltpu.SemaphoreType.DMA
    vmem = pl.BlockSpec(memory_space=pltpu.VMEM)
    anywhere = pl.BlockSpec(memory_space=pl.ANY)
    return pl.pallas_call(
        factor_kernel,
        out_shape=(
            jax.ShapeDtypeStruct((rank, rows), BF16),
            jax.ShapeDtypeStruct((4, 2, ranks, columns), BF16),
            jax.ShapeDtypeStruct((GROUP, rank), F32),
        ),
        in_specs=[vmem, anywhere],
        out_specs=(vmem, anywhere, vmem),
        scratch_shapes=[
            pltpu.VMEM((2, rows, width), BF16),
            pltpu.VMEM((CHUNKS, 4, 2, ranks, width), BF16),
            pltpu.VMEM((CHUNKS, 4, ranks, width), BF16),
            pltpu.VMEM((CHUNKS, 5, ranks, width), BF16),
            pltpu.VMEM((CHUNKS, 4, 2, ranks, width), BF16),
            pltpu.VMEM((STACK * BLOCK, BLOCK), F32),
            pltpu.VMEM((8, slice_rows, BLOCK), F32),
            pltpu.VMEM((4, STACK * BLOCK, BLOCK), F32),
            pltpu.VMEM((rank, rank), F32),
            pltpu.VMEM((2, rank, rank), BF16),
            pltpu.VMEM((rank, BLOCK), F32),
            pltpu.VMEM((4, GROUP, rank), F32),
            dma((2,)), dma((CHUNKS,)), dma((CHUNKS,)), dma((CHUNKS,)),
            dma((CHUNKS, 3)), dma((CHUNKS, 5)), dma((CHUNKS, 5)), dma((CHUNKS, 4)),
            dma((CHUNKS, 4)), dma((CHUNKS, 4)),
            dma((8,)), dma((8,)), dma((8,)), dma((8,)), dma((3,)), dma((3,)), dma((4,)), dma((4,)),
        ],
        compiler_params=pltpu.CompilerParams(
            collective_id=2, has_side_effects=True, vmem_limit_bytes=58 * 1024 * 1024
        ),
        name="factorize",
    )(pt, b)


def body(momentum, gradient, right_basis):
    pt, buffer = project(right_basis, momentum, gradient)
    ortho, right_new, sums = factorize(pt, buffer)
    rank = ortho.shape[0]
    rank_rows = right_basis.shape[0]
    right_new = right_new.reshape(rank, buffer.shape[1])
    inverse_norm = lax.rsqrt(sums[0] + epsilon)
    first = lax.axis_index("row") * rank_rows
    mine = lax.dynamic_slice_in_dim(right_new, first, rank_rows, axis=0)
    mine_norm = lax.dynamic_slice_in_dim(inverse_norm, first, rank_rows, axis=0)
    basis_next = mine.astype(F32) * mine_norm[:, None]
    scaled = (right_new.astype(F32) * inverse_norm[:, None]).astype(BF16)
    dims = (((0,), (0,)), ((), ()))
    feedback = lax.dot_general(ortho, right_new, dims, preferred_element_type=F32)
    direction = lax.dot_general(ortho, scaled, dims, preferred_element_type=F32)
    momentum_next = (buffer.astype(F32) - (1.0 - momentum_decay) * feedback).astype(BF16)
    update = (D / math.sqrt(RANK) * direction).astype(BF16)
    return (momentum_next, basis_next, update)


def solution(mesh):
    sizes = (mesh.shape["row"], mesh.shape["col"])
    return jax.shard_map(
        body if sizes == (8, 4) else plain_body,
        mesh=mesh,
        in_specs=(P("row", "col"), P("row", "col"), P("row", "col")),
        out_specs=(P("row", "col"), P("row", "col"), P("row", "col")),
        check_vma=False,
    )
```

```python
import functools
import math

import jax
import jax.numpy as jnp
from jax import lax
from jax.experimental import pallas as pl
from jax.experimental.pallas import tpu as pltpu
from jax.sharding import PartitionSpec as P

D = 16384
RANK = 1024

momentum_decay = 0.95
epsilon = 1e-06

BLOCK = 128
GROUP = 8
PACK = 256

HIGHEST = lax.Precision.HIGHEST


def across(x, column):
    return jnp.broadcast_to(x[:, column : column + 1], (x.shape[0], BLOCK))


def down(x, row):
    return jnp.broadcast_to(x[row : row + 1, :], (GROUP, BLOCK))


def factor_block(block):
    groups = BLOCK // GROUP
    sub = lax.broadcasted_iota(jnp.int32, (GROUP, BLOCK), 0)
    lane = lax.broadcasted_iota(jnp.int32, (GROUP, BLOCK), 1)
    left = [block[GROUP * g : GROUP * (g + 1), :] for g in range(groups)]
    right = [jnp.where(lane == sub + GROUP * g, 1.0, 0.0) for g in range(groups)]
    inverse = []
    for g in range(groups):
        first = GROUP * g
        jordan_left, jordan_right = left[g], right[g]
        columns = [across(jordan_left, first + l) for l in range(GROUP)]
        forward_right, pivots = jordan_right, jnp.ones_like(jordan_left)
        for l in range(GROUP):
            pivot = down(columns[l], l)
            reciprocal = 1.0 / pivot
            mine = sub == l
            column = columns[l]
            row_left, row_right = down(jordan_left, l), down(jordan_right, l)
            forward_right = jnp.where(mine, row_right, forward_right)
            pivots = jnp.where(mine, pivot, pivots)
            row_left, row_right = row_left * reciprocal, row_right * reciprocal
            jordan_left = jnp.where(mine, row_left, jordan_left - column * row_left)
            jordan_right = jnp.where(mine, row_right, jordan_right - column * row_right)
            for m in range(l + 1, GROUP):
                row = down(columns[m], l) * reciprocal
                columns[m] = jnp.where(mine, row, columns[m] - column * row)
        inverse.append(forward_right * lax.rsqrt(pivots))
        rows_left = [down(jordan_left, l) for l in range(GROUP)]
        rows_right = [down(jordan_right, l) for l in range(GROUP)]
        for h in range(g + 1, groups):
            base = left[h]
            new_left, new_right = base, right[h]
            for l in range(GROUP):
                coefficient = across(base, first + l)
                new_left = new_left - coefficient * rows_left[l]
                new_right = new_right - coefficient * rows_right[l]
            left[h], right[h] = new_left, new_right
    return jnp.concatenate(inverse, axis=0)


def plain_factor_kernel(packed_ref, share_ref, ortho_ref, work):
    rank = work.shape[0]
    blocks = rank // BLOCK
    offset = 0
    for i in range(rank // PACK):
        for j in range(i + 1):
            tile = packed_ref[:, offset : offset + PACK]
            offset += PACK
            work[PACK * i : PACK * (i + 1), PACK * j : PACK * (j + 1)] = tile
            if j < i:
                work[PACK * j : PACK * (j + 1), PACK * i : PACK * (i + 1)] = tile.T
    column_block = lax.broadcasted_iota(jnp.int32, (BLOCK, rank), 1) // BLOCK

    def step(k, carry):
        here = pl.ds(pl.multiple_of(k * BLOCK, BLOCK), BLOCK)
        x = factor_block(work[here, here])
        pivot_rows = jnp.dot(x, work[here, :], precision=HIGHEST, preferred_element_type=jnp.float32)
        wide = jnp.concatenate([x] * blocks, axis=1)
        pivot_rows = jnp.where(column_block == k, wide, pivot_rows)
        work[here, :] = pivot_rows

        def below(i, carry):
            there = pl.ds(pl.multiple_of(i * BLOCK, BLOCK), BLOCK)
            panel = lax.dot_general(
                work[there, here], x, (((1,), (1,)), ((), ())),
                precision=HIGHEST, preferred_element_type=jnp.float32,
            )
            work[there, here] = jnp.zeros((BLOCK, BLOCK), jnp.float32)
            work[there, :] = work[there, :] - jnp.dot(
                panel, work[here, :], precision=HIGHEST, preferred_element_type=jnp.float32
            )
            return carry

        lax.fori_loop(k + 1, blocks, below, 0)
        rest = jnp.where(column_block <= k, pivot_rows, 0.0)
        total = jnp.zeros((share_ref.shape[0], BLOCK), jnp.float32)
        for _ in range(3):
            part = rest.astype(jnp.bfloat16)
            rest = rest - part.astype(jnp.float32)
            total = total + lax.dot_general(
                share_ref[...], part, (((1,), (1,)), ((), ())),
                preferred_element_type=jnp.float32,
            )
        ortho_ref[:, here] = total.astype(jnp.bfloat16)
        return carry

    lax.fori_loop(0, blocks, step, 0)


def orthonormalize(row_share, packed):
    rank = row_share.shape[1]
    return pl.pallas_call(
        plain_factor_kernel,
        out_shape=jax.ShapeDtypeStruct(row_share.shape, jnp.bfloat16),
        in_specs=[pl.BlockSpec(memory_space=pltpu.VMEM)] * 2,
        out_specs=pl.BlockSpec(memory_space=pltpu.VMEM),
        scratch_shapes=[pltpu.VMEM((rank, rank), jnp.float32)],
        compiler_params=pltpu.CompilerParams(vmem_limit_bytes=40 * 1024 * 1024),
        name="factor",
    )(packed, row_share)


def packed_gram(share):
    pieces = []
    for i in range(share.shape[1] // PACK):
        pieces.append(
            lax.dot_general(
                share[:, PACK * i : PACK * (i + 1)],
                share[:, : PACK * (i + 1)],
                (((0,), (0,)), ((), ())),
                preferred_element_type=jnp.float32,
            )
        )
    return jnp.concatenate(pieces, axis=1)


def plain_body(momentum, gradient, right_basis):
    buffer = (momentum.astype(jnp.float32) + gradient.astype(jnp.float32)).astype(jnp.bfloat16)
    rank_rows = right_basis.shape[0]
    partial_value = lax.dot_general(
        buffer,
        lax.all_gather(right_basis, "row", axis=0, tiled=True),
        (((1,), (1,)), ((), ())),
        preferred_element_type=jnp.float32,
    )
    row_share = lax.psum_scatter(
        partial_value.astype(jnp.bfloat16), "col", scatter_dimension=0, tiled=True
    )
    packed = lax.psum(packed_gram(row_share), ("row", "col"))
    ortho_share = orthonormalize(row_share, packed)
    orthonormal = lax.all_gather(ortho_share, "col", axis=0, tiled=True)
    right_share = lax.psum_scatter(
        lax.dot_general(
            orthonormal, buffer, (((0,), (0,)), ((), ())), preferred_element_type=jnp.float32
        ).astype(jnp.bfloat16),
        "row",
        scatter_dimension=0,
        tiled=True,
    )
    gathered = lax.all_gather(right_share, "row", axis=0, tiled=True)
    right_wide = right_share.astype(jnp.float32)
    sums = jnp.sum(right_wide * right_wide, axis=1)
    everyone = lax.all_gather(sums, ("row", "col"), axis=0)
    everyone = everyone.reshape(lax.axis_size("row"), lax.axis_size("col"), rank_rows)
    inverse_rows = lax.rsqrt(jnp.sum(everyone, axis=1) + epsilon)
    inverse_norm = inverse_rows.reshape(-1, 1)
    mine = lax.dynamic_index_in_dim(inverse_rows, lax.axis_index("row"), 0, keepdims=False)
    basis_next = right_wide * mine[:, None]
    scaled = (gathered.astype(jnp.float32) * inverse_norm).astype(jnp.bfloat16)
    feedback = jnp.dot(orthonormal, gathered, preferred_element_type=jnp.float32)
    direction = jnp.dot(orthonormal, scaled, preferred_element_type=jnp.float32)
    momentum_next = (buffer.astype(jnp.float32) - (1.0 - momentum_decay) * feedback).astype(
        jnp.bfloat16
    )
    update_scale = D / math.sqrt(RANK)
    update = (update_scale * direction).astype(jnp.bfloat16)
    return (momentum_next, basis_next, update)


MESH = pl.DeviceIdType.MESH
CHUNKS = 4
STACK = 9
F32 = jnp.float32
BF16 = jnp.bfloat16


def remote(src, dst, send_sem, recv_sem, device):
    return pltpu.make_async_remote_copy(
        src_ref=src, dst_ref=dst, send_sem=send_sem, recv_sem=recv_sem,
        device_id=device, device_id_type=MESH,
    )


def places():
    row, col = lax.axis_index("row"), lax.axis_index("col")
    return row, col, row // 2, lax.rem(row, 2), col // 2, lax.rem(col, 2)


def greet(devices):
    barrier = pltpu.get_barrier_semaphore()
    for device in devices:
        pl.semaphore_signal(barrier, inc=1, device_id=device, device_id_type=MESH)
    pl.semaphore_wait(barrier, len(devices))


def nt_dot(a, b):
    return lax.dot_general(a, b, (((1,), (1,)), ((), ())), preferred_element_type=F32)


def project_kernel(
    v_ref, m_hbm, g_hbm, pt_ref, b_hbm,
    buf, basis, m_tile, g_tile, part, core_in, half, y_in,
    load_sem, store_sem, own_send, hop_send, x_send, z_recv, x_recv,
    core_send, core_recv, y_send, y_recv, share_send, share_recv,
):
    row, col, z, x, y, k = places()
    rows = buf.shape[0]
    tile = m_tile.shape[1]
    tiles = rows // tile
    x_peer = (z * 2 + 1 - x, col)
    core_peer = (row, y * 2 + 1 - k)
    y_peer = (row, (1 - y) * 2 + k)
    middle = jnp.logical_and(z > 0, z < 3)
    order = [z, jnp.bitwise_xor(z, 1), jnp.where(z < 2, 2, 1), jnp.where(z < 2, 3, 0)]

    def load(i, slot):
        here = pl.ds(pl.multiple_of(i * tile, tile), tile)
        return (
            pltpu.make_async_copy(m_hbm.at[here], m_tile.at[slot], load_sem.at[0, slot]),
            pltpu.make_async_copy(g_hbm.at[here], g_tile.at[slot], load_sem.at[1, slot]),
        )

    for slot in range(2):
        for copy in load(slot, slot):
            copy.start()
    greet(
        [(lax.rem(z + 1, 4) * 2 + x, col), (lax.rem(z + 2, 4) * 2 + x, col), (lax.rem(z + 3, 4) * 2 + x, col)]
        + [x_peer, core_peer, y_peer]
    )
    own_up = remote(v_ref, basis.at[z, x], own_send.at[0], z_recv.at[z], (jnp.minimum(z + 1, 3) * 2 + x, col))
    own_down = remote(v_ref, basis.at[z, x], own_send.at[1], z_recv.at[z], (jnp.maximum(z - 1, 0) * 2 + x, col))
    own_side = remote(v_ref, basis.at[z, x], x_send.at[z], x_recv.at[z], x_peer)

    @pl.when(z < 3)
    def _():
        own_up.start()

    @pl.when(z > 0)
    def _():
        own_down.start()

    own_side.start()
    basis[z, x] = v_ref[...]

    def build(i, carry):
        slot = lax.rem(i, 2)
        for copy in load(i, slot):
            copy.wait()
        here = pl.ds(pl.multiple_of(i * tile, tile), tile)
        buf[here, :] = (m_tile[slot].astype(F32) + g_tile[slot].astype(F32)).astype(BF16)

        @pl.when(i + 2 < tiles)
        def _():
            for copy in load(i + 2, slot):
                copy.start()

        return carry

    lax.fori_loop(0, tiles, build, 0)
    store = pltpu.make_async_copy(buf, b_hbm, store_sem)
    store.start()

    def hop(s):
        q = order[s]
        target = jnp.where(z == 1, jnp.where(q < z, 2, 0), jnp.where(q < z, 3, 1))
        return remote(basis.at[q, x], basis.at[q, x], hop_send.at[s - 1], z_recv.at[q], (target * 2 + x, col))

    def side(s):
        q = order[s]
        return remote(basis.at[q, x], basis.at[q, x], x_send.at[q], x_recv.at[q], x_peer)

    def take(s):
        hop(s).wait_recv()

        @pl.when(middle)
        def _():
            hop(s).start()

        side(s).start()

    def side_in(s):
        q = order[s]
        remote(basis.at[q, x], basis.at[q, 1 - x], x_send.at[q], x_recv.at[q], x_peer).wait_recv()

    def to_core(s):
        return remote(part.at[s, 1 - k], core_in.at[s], core_send.at[s], core_recv.at[s], core_peer)

    def to_y(s):
        return remote(half.at[s], y_in.at[s], y_send.at[s], y_recv.at[s], y_peer)

    def share(s):
        return remote(pt_ref.at[order[s], k], pt_ref.at[order[s], k], share_send.at[s], share_recv.at[s], core_peer)

    def share_in(s):
        return remote(pt_ref.at[order[s], k], pt_ref.at[order[s], 1 - k], share_send.at[s], share_recv.at[s], core_peer)

    def multiply(s):
        q = order[s]
        width = 512

        def columns(n, carry):
            here = pl.ds(pl.multiple_of(n * width, width), width)
            left = basis[q].reshape(2 * basis.shape[2], basis.shape[3])
            value = nt_dot(left, buf[here, :])
            part[s, :, :, here] = value.astype(BF16).reshape(2, basis.shape[2], width)
            return carry

        lax.fori_loop(0, rows // width, columns, 0)
        to_core(s).start()

    def add_core(s):
        to_core(s).wait_recv()
        half[s] = (part[s, k].astype(F32) + core_in[s].astype(F32)).astype(BF16)
        to_y(s).start()

    def add_y(s):
        to_y(s).wait_recv()
        pt_ref[order[s], k] = (half[s].astype(F32) + y_in[s].astype(F32)).astype(BF16)
        share(s).start()

    take(1)

    @pl.when(middle)
    def _():
        take(2)

    side_in(0)
    multiply(0)

    @pl.when(jnp.logical_not(middle))
    def _():
        take(2)

    add_core(0)

    @pl.when(middle)
    def _():
        take(3)

    side_in(1)
    multiply(1)
    add_y(0)
    add_core(1)

    @pl.when(jnp.logical_not(middle))
    def _():
        take(3)

    side_in(2)
    multiply(2)
    add_y(1)
    add_core(2)
    side_in(3)
    multiply(3)
    add_y(2)
    add_core(3)
    add_y(3)

    @pl.when(z < 3)
    def _():
        own_up.wait_send()

    @pl.when(z > 0)
    def _():
        own_down.wait_send()

    own_side.wait_send()

    @pl.when(middle)
    def _():
        for s in range(1, 4):
            hop(s).wait_send()

    for s in range(1, 4):
        side(s).wait_send()
    for s in range(4):
        to_core(s).wait_send()
        to_y(s).wait_send()
        share(s).wait_send()
        share_in(s).wait_recv()
    store.wait()


def project(v, m, g):
    rows, columns = m.shape
    ranks = v.shape[0]
    dma = pltpu.SemaphoreType.DMA
    vmem = pl.BlockSpec(memory_space=pltpu.VMEM)
    anywhere = pl.BlockSpec(memory_space=pl.ANY)
    return pl.pallas_call(
        project_kernel,
        out_shape=(
            jax.ShapeDtypeStruct((4, 2, ranks, rows), BF16),
            jax.ShapeDtypeStruct((rows, columns), BF16),
        ),
        in_specs=[vmem, anywhere, anywhere],
        out_specs=(vmem, anywhere),
        scratch_shapes=[
            pltpu.VMEM((rows, columns), BF16),
            pltpu.VMEM((4, 2, ranks, columns), BF16),
            pltpu.VMEM((2, 128, columns), BF16),
            pltpu.VMEM((2, 128, columns), BF16),
            pltpu.VMEM((4, 2, ranks, rows), BF16),
            pltpu.VMEM((4, ranks, rows), BF16),
            pltpu.VMEM((4, ranks, rows), BF16),
            pltpu.VMEM((4, ranks, rows), BF16),
            dma((2, 2)), dma, dma((2,)), dma((3,)), dma((4,)), dma((4,)), dma((4,)),
            dma((4,)), dma((4,)), dma((4,)), dma((4,)), dma((4,)), dma((4,)),
        ],
        compiler_params=pltpu.CompilerParams(
            collective_id=1, has_side_effects=True, vmem_limit_bytes=58 * 1024 * 1024
        ),
        cost_estimate=pl.CostEstimate(flops=2 * rows * columns * ranks * 8, bytes_accessed=6 * rows * columns, transcendentals=0),
        name="project",
    )(v, m, g)


def factor_kernel(
    pt_ref, b_hbm, o_ref, n_hbm, m_hbm, sums_ref,
    buf, wpart, x_in, z_in, whole, stack, stack_in, stack_all, work, inverse, squares, norm_in,
    load_sem, store_sem, back_sem, xs, xr, zs, zr, gs, gr, fs, ys,
    ss, sr, ts, tr, us, ur, ns, nr,
):
    row, col, z, x, y, k = places()
    ranks = pt_ref.shape[2]
    rank = work.shape[0]
    blocks = rank // BLOCK
    chunks = wpart.shape[0]
    width = wpart.shape[4]
    slice_rows = stack_in.shape[1]
    x_peer = (z * 2 + 1 - x, col)
    core_peer = (row, y * 2 + 1 - k)
    y_peer = (row, (1 - y) * 2 + k)

    def z_of(shift):
        return lax.rem(z + shift, 4)

    def z_peer(shift):
        return (z_of(shift) * 2 + x, col)

    def row_of(shift):
        return lax.rem(row + shift, 8)

    def load(j):
        return pltpu.make_async_copy(
            b_hbm.at[:, pl.ds(j * width, width)], buf.at[j % 2], load_sem.at[j % 2]
        )

    load(0).start()
    load(1).start()
    greet([(row_of(shift), col) for shift in range(1, 8)] + [core_peer, y_peer])

    def gram(t, carry):
        early = t < 8 - col
        i = jnp.where(early, col + t, t - 1)
        j = jnp.where(early, col, 7 - col)
        value = nt_dot(pt_ref[i // 2, lax.rem(i, 2)], pt_ref[j // 2, lax.rem(j, 2)])
        stack[pl.ds(pl.multiple_of(t * BLOCK, BLOCK), BLOCK), :] = value
        return carry

    lax.fori_loop(0, STACK, gram, 0)

    def part_of(r):
        return pl.ds(pl.multiple_of(r * slice_rows, slice_rows), slice_rows)

    def gram_out(shift):
        to = row_of(shift)
        return remote(stack.at[part_of(to)], stack_in.at[row], ss.at[shift], sr.at[row], (to, col))

    def gram_in(shift):
        who = row_of(shift)
        return remote(stack.at[part_of(row)], stack_in.at[who], ss.at[shift], sr.at[who], (who, col))

    def sum_out(shift):
        to = row_of(shift)
        return remote(stack_all.at[col, part_of(row)], stack_all.at[col, part_of(row)], ts.at[shift], tr.at[row], (to, col))

    def sum_in(shift):
        who = row_of(shift)
        return remote(stack_all.at[col, part_of(who)], stack_all.at[col, part_of(who)], ts.at[shift], tr.at[who], (who, col))

    def spread(index, what, device):
        return remote(stack_all.at[what], stack_all.at[what], us.at[index], ur.at[index], device)

    for shift in range(1, 8):
        gram_out(shift).start()

    def side_out(j):
        return remote(wpart.at[j, :, 1 - x], x_in.at[j], xs.at[j], xr.at[j], x_peer)

    def weigh(j, which):
        step = 256

        def columns(n, carry):
            here = pl.ds(pl.multiple_of(n * step, step), step)
            left = pt_ref[:, which].reshape(4 * ranks, pt_ref.shape[3])
            value = jnp.dot(left, buf[j % 2, :, here], preferred_element_type=F32)
            wpart[j, :, which, :, here] = value.astype(BF16).reshape(4, ranks, step)
            return carry

        lax.fori_loop(0, width // step, columns, 0)

    def product(j):
        load(j).wait()
        weigh(j, 1 - x)
        if j < 1:
            side_out(j).start()
        weigh(j, x)
        if j + 2 < chunks:
            load(j + 2).start()

    end = jnp.logical_or(z == 0, z == 3)
    low = z < 2

    def line_send(j, i, piece, to, slot):
        return remote(x_in.at[j, piece], z_in.at[j, slot], zs.at[j, i], zr.at[j, slot], (to * 2 + x, col))

    def line_take(j, slot):
        remote(x_in.at[j, 0], z_in.at[j, slot], zs.at[j, 0], zr.at[j, slot], x_peer).wait_recv()

    def line_first(j):
        for i in range(3):
            piece = jnp.where(low, 3 - i, i)
            slot = piece if i < 2 else jnp.where(low, 1, 4)
            line_send(j, i, piece, jnp.where(low, 1, 2), slot).start()

    def add_in(j, piece):
        line_take(j, piece)
        x_in[j, piece] = (x_in[j, piece].astype(F32) + z_in[j, piece].astype(F32)).astype(BF16)

    def add_side(j):
        side_out(j).wait_recv()
        if j + 1 < chunks:
            side_out(j + 1).start()
        for shift in (1, 2, 3, 0):
            there = z_of(shift)
            x_in[j, there] = (wpart[j, there, x].astype(F32) + x_in[j, there].astype(F32)).astype(BF16)

        @pl.when(end)
        def _():
            line_first(j)

    def line_second(j):
        @pl.when(jnp.logical_not(end))
        def _():
            for i in range(2):
                piece = jnp.where(low, 3 - i, i)
                slot = piece if i < 1 else jnp.where(low, 2, 4)
                add_in(j, piece)
                line_send(j, i, piece, jnp.where(low, 2, 1), slot).start()

    def line_third(j):
        @pl.when(jnp.logical_not(end))
        def _():
            piece = jnp.where(low, 0, 3)
            add_in(j, piece)
            line_send(j, 2, piece, piece, jnp.where(low, 4, 3)).start()

    order = [z, jnp.bitwise_xor(z, 1), jnp.where(low, 2, 1), jnp.where(low, 3, 0)]

    def full_send(j, q, sem, to):
        return remote(whole.at[j, q, x], whole.at[j, q, x], gs.at[j, sem], gr.at[j, q], (to * 2 + x, col))

    def own_up(j):
        return full_send(j, z, 0, jnp.minimum(z + 1, 3))

    def own_down(j):
        return full_send(j, z, 1, jnp.maximum(z - 1, 0))

    def hop(j, s):
        q = order[s]
        return full_send(j, q, s + 1, jnp.where(low, jnp.where(q < z, 2, 0), jnp.where(q < z, 3, 1)))

    def full_side(j, q):
        return remote(whole.at[j, q, x], whole.at[j, q, x], fs.at[j, q], ys.at[j, q], x_peer)

    def full_side_in(j, q):
        return remote(whole.at[j, q, x], whole.at[j, q, 1 - x], fs.at[j, q], ys.at[j, q], x_peer)

    def finish(j):
        @pl.when(z > 0)
        def _():
            line_take(j, z)
            x_in[j, z] = (x_in[j, z].astype(F32) + z_in[j, z].astype(F32)).astype(BF16)

        @pl.when(z < 3)
        def _():
            line_take(j, 4)
            x_in[j, z] = (x_in[j, z].astype(F32) + z_in[j, 4].astype(F32)).astype(BF16)

        whole[j, z, x] = x_in[j, z]

        @pl.when(z < 3)
        def _():
            own_up(j).start()

        @pl.when(z > 0)
        def _():
            own_down(j).start()

        full_side(j, z).start()

    def take(j, s):
        hop(j, s).wait_recv()

        @pl.when(jnp.logical_not(end))
        def _():
            hop(j, s).start()

        full_side(j, order[s]).start()

    def take_first(j):
        take(j, 1)

        @pl.when(jnp.logical_not(end))
        def _():
            take(j, 2)

    def take_second(j):
        @pl.when(end)
        def _():
            take(j, 2)

    def take_third(j):
        take(j, 3)

    def sum_gram():
        total = stack[part_of(row), :]
        for shift in range(1, 8):
            gram_in(shift).wait_recv()
            total = total + stack_in[row_of(shift)]
        stack_all[col, part_of(row), :] = total
        for shift in range(1, 8):
            sum_out(shift).start()

    other_col = (1 - y) * 2 + k

    def spread_gram():
        for shift in range(1, 8):
            sum_in(shift).wait_recv()
        spread(1, col, y_peer).start()
        spread(0, col, core_peer).start()

    def end_gram():
        spread(1, other_col, y_peer).wait_recv()
        spread(2, other_col, core_peer).start()
        spread(0, y * 2 + 1 - k, core_peer).wait_recv()
        spread(2, (1 - y) * 2 + 1 - k, core_peer).wait_recv()

    product(0)
    product(1)
    product(2)
    product(3)
    add_side(0)
    line_second(0)
    sum_gram()
    add_side(1)
    line_third(0)
    finish(0)
    spread_gram()
    line_second(1)
    line_third(1)
    add_side(2)
    take_first(0)
    finish(1)
    end_gram()
    line_second(2)

    for c in range(4):
        for t in range(STACK):
            i, j = (c + t, c) if t < 8 - c else (t - 1, 7 - c)
            value = stack_all[c, BLOCK * t : BLOCK * (t + 1), :]
            work[BLOCK * i : BLOCK * (i + 1), BLOCK * j : BLOCK * (j + 1)] = value
            if i != j:
                work[BLOCK * j : BLOCK * (j + 1), BLOCK * i : BLOCK * (i + 1)] = value.T

    column_block = lax.broadcasted_iota(jnp.int32, (BLOCK, rank), 1) // BLOCK
    events = {
        0: [(add_side, 3), (line_third, 2)],
        1: [(take_first, 1), (finish, 2)],
        2: [(line_second, 3)],
        3: [(take_second, 1), (take_first, 2), (line_third, 3), (take_second, 0), (take_second, 2)],
        4: [(finish, 3)],
        5: [(take_third, 0)],
        6: [(take_third, 1), (take_third, 2), (take_first, 3)],
        7: [],
    }

    def step(kk, carry):
        here = pl.ds(pl.multiple_of(kk * BLOCK, BLOCK), BLOCK)
        factor = factor_block(work[here, here])
        pivot_rows = jnp.dot(factor, work[here, :], precision=HIGHEST, preferred_element_type=F32)
        wide = jnp.concatenate([factor] * blocks, axis=1)
        pivot_rows = jnp.where(column_block == kk, wide, pivot_rows)
        work[here, :] = pivot_rows

        def below(i, carry):
            there = pl.ds(pl.multiple_of(i * BLOCK, BLOCK), BLOCK)
            panel = lax.dot_general(
                work[there, here], factor, (((1,), (1,)), ((), ())),
                precision=HIGHEST, preferred_element_type=F32,
            )
            work[there, here] = jnp.zeros((BLOCK, BLOCK), F32)
            work[there, :] = work[there, :] - jnp.dot(
                panel, work[here, :], precision=HIGHEST, preferred_element_type=F32
            )
            return carry

        lax.fori_loop(kk + 1, blocks, below, 0)
        rest = jnp.where(column_block <= kk, pivot_rows, 0.0)
        high = rest.astype(BF16)
        inverse[0, here, :] = high
        inverse[1, here, :] = (rest - high.astype(F32)).astype(BF16)
        for at, todo in events.items():
            if todo:
                @pl.when(kk == at)
                def _(todo=todo):
                    for function, j in todo:
                        function(j)
        return carry

    lax.fori_loop(0, blocks, step, 0)

    def apply(load_right, store_out, columns):
        tile = 512

        def one(n, carry):
            here = pl.ds(pl.multiple_of(n * tile, tile), tile)
            right = load_right(here)
            for i in range(4):
                rows = slice(256 * i, 256 * (i + 1))
                deep = 256 * (i + 1)
                left = inverse[:, rows, :deep].reshape(512, deep)
                value = jnp.dot(left, right[:deep], preferred_element_type=F32)
                store_out(i, here, value[:256] + value[256:])
            return carry

        lax.fori_loop(0, columns // tile, one, 0)

    def p_load(here):
        return pt_ref[:, :, :, here].reshape(rank, 512)

    def o_store(i, here, value):
        o_ref[here, 256 * i : 256 * (i + 1)] = value.T.astype(BF16)

    load(0).start()
    load(1).start()
    apply(p_load, o_store, pt_ref.shape[3])
    squares[...] = jnp.zeros_like(squares)

    def store(j):
        return pltpu.make_async_copy(
            wpart.at[j], n_hbm.at[:, :, :, pl.ds(j * width, width)], store_sem.at[j]
        )

    def back(j):
        return pltpu.make_async_copy(
            buf.at[j % 2], m_hbm.at[:, pl.ds(j * width, width)], back_sem.at[j % 2]
        )

    def right(j):
        for q in range(4):
            full_side_in(j, q).wait_recv()
        side_out(j).wait_send()

        def w_load(here):
            return whole[j, :, :, :, here].reshape(rank, 512)

        def n_store(i, here, value):
            low = value.astype(BF16)
            wpart[j, i, :, :, here] = low.reshape(2, ranks, 512)
            low = low.astype(F32)
            low = low * low
            squares[256 * i : 256 * (i + 1), :] += sum(
                low[:, BLOCK * g : BLOCK * (g + 1)] for g in range(1, 4)
            ) + low[:, :BLOCK]

        apply(w_load, n_store, width)
        store(j).start()

    def feed_back(j):
        load(j).wait()
        tall, wide = 512, 512

        def one(t, carry):
            across_tiles = width // wide
            rows = pl.ds(pl.multiple_of(t // across_tiles * tall, tall), tall)
            here = pl.ds(pl.multiple_of(lax.rem(t, across_tiles) * wide, wide), wide)
            value = jnp.dot(
                o_ref[rows, :], wpart[j, :, :, :, here].reshape(rank, wide), preferred_element_type=F32
            )
            old = buf[j % 2, rows, here].astype(F32)
            buf[j % 2, rows, here] = (old - (1.0 - momentum_decay) * value).astype(BF16)
            return carry

        lax.fori_loop(0, buf.shape[1] // tall * (width // wide), one, 0)
        back(j).start()
        if j + 2 < chunks:
            back(j).wait()
            load(j + 2).start()

    right(0)
    take_second(3)
    feed_back(0)
    right(1)
    feed_back(1)
    take_third(3)
    right(2)
    feed_back(2)
    right(3)

    def norm(shift):
        to = lax.rem(col + shift, 4)
        return remote(norm_in.at[col], norm_in.at[col], ns.at[shift], nr.at[col], (row, to))

    def norm_from(shift):
        who = lax.rem(col + shift, 4)
        return remote(norm_in.at[who], norm_in.at[who], ns.at[shift], nr.at[who], (row, who))

    ones = jnp.ones((GROUP, BLOCK), F32)
    norm_in[col] = lax.dot_general(
        ones, squares[...], (((1,), (1,)), ((), ())), precision=HIGHEST, preferred_element_type=F32
    )
    for shift in range(1, 4):
        norm(shift).start()
    feed_back(3)
    for shift in range(1, 4):
        norm_from(shift).wait_recv()
    sums_ref[...] = (norm_in[0] + norm_in[1]) + (norm_in[2] + norm_in[3])
    for shift in range(1, 4):
        norm(shift).wait_send()
    for shift in range(1, 8):
        gram_out(shift).wait_send()
        sum_out(shift).wait_send()
    spread(0, col, core_peer).wait_send()
    spread(1, col, y_peer).wait_send()
    spread(2, other_col, core_peer).wait_send()
    for j in range(chunks):
        for i in range(3):
            line_send(j, i, 0, z, 0).wait_send()

        @pl.when(z < 3)
        def _():
            own_up(j).wait_send()

        @pl.when(z > 0)
        def _():
            own_down(j).wait_send()

        @pl.when(jnp.logical_not(end))
        def _():
            for s in range(1, 4):
                hop(j, s).wait_send()

        for q in range(4):
            full_side(j, q).wait_send()
        store(j).wait()
    back(chunks - 2).wait()
    back(chunks - 1).wait()


def factorize(pt, b):
    _, _, ranks, rows = pt.shape
    columns = b.shape[1]
    rank = 8 * ranks
    width = columns // CHUNKS
    slice_rows = STACK * BLOCK // 8
    dma = pltpu.SemaphoreType.DMA
    vmem = pl.BlockSpec(memory_space=pltpu.VMEM)
    anywhere = pl.BlockSpec(memory_space=pl.ANY)
    return pl.pallas_call(
        factor_kernel,
        out_shape=(
            jax.ShapeDtypeStruct((rows, rank), BF16),
            jax.ShapeDtypeStruct((4, 2, ranks, columns), BF16),
            jax.ShapeDtypeStruct((rows, columns), BF16),
            jax.ShapeDtypeStruct((GROUP, rank), F32),
        ),
        in_specs=[vmem, anywhere],
        out_specs=(vmem, anywhere, anywhere, vmem),
        scratch_shapes=[
            pltpu.VMEM((2, rows, width), BF16),
            pltpu.VMEM((CHUNKS, 4, 2, ranks, width), BF16),
            pltpu.VMEM((CHUNKS, 4, ranks, width), BF16),
            pltpu.VMEM((CHUNKS, 5, ranks, width), BF16),
            pltpu.VMEM((CHUNKS, 4, 2, ranks, width), BF16),
            pltpu.VMEM((STACK * BLOCK, BLOCK), F32),
            pltpu.VMEM((8, slice_rows, BLOCK), F32),
            pltpu.VMEM((4, STACK * BLOCK, BLOCK), F32),
            pltpu.VMEM((rank, rank), F32),
            pltpu.VMEM((2, rank, rank), BF16),
            pltpu.VMEM((rank, BLOCK), F32),
            pltpu.VMEM((4, GROUP, rank), F32),
            dma((2,)), dma((CHUNKS,)), dma((2,)), dma((CHUNKS,)), dma((CHUNKS,)),
            dma((CHUNKS, 3)), dma((CHUNKS, 5)), dma((CHUNKS, 5)), dma((CHUNKS, 4)),
            dma((CHUNKS, 4)), dma((CHUNKS, 4)),
            dma((8,)), dma((8,)), dma((8,)), dma((8,)), dma((3,)), dma((3,)), dma((4,)), dma((4,)),
        ],
        compiler_params=pltpu.CompilerParams(
            collective_id=2, has_side_effects=True, vmem_limit_bytes=58 * 1024 * 1024
        ),
        name="factorize",
    )(pt, b)


def update_kernel(o_ref, n_ref, m_ref, sums_ref, m_out, basis_ref, update_ref, inverse, scaled):
    ranks = basis_ref.shape[0]

    @pl.when(pl.program_id(0) == 0)
    def _():
        norm = lax.rsqrt(sums_ref[0:1, :] + epsilon)
        inverse[...] = jnp.broadcast_to(norm, (BLOCK, norm.shape[1])).T

    m_out[...] = m_ref[...]
    width = n_ref.shape[1]
    wide = jnp.concatenate([inverse[...]] * (width // BLOCK), axis=1)
    scaled[...] = (n_ref[...].astype(F32) * wide).astype(BF16)
    mine = pl.ds(pl.multiple_of(lax.axis_index("row") * ranks, ranks), ranks)
    own = jnp.concatenate([inverse[mine, :]] * (width // BLOCK), axis=1)
    basis_ref[...] = n_ref[mine, :].astype(F32) * own
    tall = 512

    def one(t, carry):
        rows = pl.ds(pl.multiple_of(t * tall, tall), tall)
        value = jnp.dot(o_ref[rows, :], scaled[...], preferred_element_type=F32)
        update_ref[rows, :] = (D / math.sqrt(RANK) * value).astype(BF16)
        return carry

    lax.fori_loop(0, o_ref.shape[0] // tall, one, 0)


def finish_update(ortho, right_new, momentum_next, sums, ranks):
    rows, columns = momentum_next.shape
    rank = ortho.shape[1]
    width = 512

    def strip(height):
        return pl.BlockSpec((height, width), lambda j: (0, j))

    def fixed(shape):
        return pl.BlockSpec(shape, lambda j: (0, 0))

    return pl.pallas_call(
        update_kernel,
        grid=(columns // width,),
        out_shape=(
            jax.ShapeDtypeStruct((rows, columns), BF16),
            jax.ShapeDtypeStruct((ranks, columns), F32),
            jax.ShapeDtypeStruct((rows, columns), BF16),
        ),
        in_specs=[fixed((rows, rank)), strip(rank), strip(rows), fixed((GROUP, rank))],
        out_specs=(strip(rows), strip(ranks), strip(rows)),
        scratch_shapes=[pltpu.VMEM((rank, BLOCK), F32), pltpu.VMEM((rank, width), BF16)],
        compiler_params=pltpu.CompilerParams(vmem_limit_bytes=58 * 1024 * 1024),
        cost_estimate=pl.CostEstimate(flops=2 * rows * columns * rank, bytes_accessed=8 * rows * columns, transcendentals=0),
        name="update",
    )(ortho, right_new, momentum_next, sums)


def body(momentum, gradient, right_basis):
    pt, buffer = project(right_basis, momentum, gradient)
    ortho, right_new, momentum_next, sums = factorize(pt, buffer)
    right_new = right_new.reshape(ortho.shape[1], buffer.shape[1])
    return finish_update(ortho, right_new, momentum_next, sums, right_basis.shape[0])


def solution(mesh):
    sizes = (mesh.shape["row"], mesh.shape["col"])
    return jax.shard_map(
        body if sizes == (8, 4) else plain_body,
        mesh=mesh,
        in_specs=(P("row", "col"), P("row", "col"), P("row", "col")),
        out_specs=(P("row", "col"), P("row", "col"), P("row", "col")),
        check_vma=False,
    )
```

```python
import functools
import math

import jax
import jax.numpy as jnp
from jax import lax
from jax.experimental import pallas as pl
from jax.experimental.pallas import tpu as pltpu
from jax.sharding import PartitionSpec as P

D = 16384
RANK = 1024

momentum_decay = 0.95
epsilon = 1e-06

BLOCK = 128
GROUP = 8
PACK = 256

HIGHEST = lax.Precision.HIGHEST


def across(x, column):
    return jnp.broadcast_to(x[:, column : column + 1], (x.shape[0], BLOCK))


def down(x, row):
    return jnp.broadcast_to(x[row : row + 1, :], (GROUP, BLOCK))


def factor_block(block):
    groups = BLOCK // GROUP
    sub = lax.broadcasted_iota(jnp.int32, (GROUP, BLOCK), 0)
    lane = lax.broadcasted_iota(jnp.int32, (GROUP, BLOCK), 1)
    left = [block[GROUP * g : GROUP * (g + 1), :] for g in range(groups)]
    right = [jnp.where(lane == sub + GROUP * g, 1.0, 0.0) for g in range(groups)]
    inverse = []
    for g in range(groups):
        first = GROUP * g
        jordan_left, jordan_right = left[g], right[g]
        columns = [across(jordan_left, first + l) for l in range(GROUP)]
        forward_right, pivots = jordan_right, jnp.ones_like(jordan_left)
        for l in range(GROUP):
            pivot = down(columns[l], l)
            reciprocal = 1.0 / pivot
            mine = sub == l
            column = columns[l]
            row_left, row_right = down(jordan_left, l), down(jordan_right, l)
            forward_right = jnp.where(mine, row_right, forward_right)
            pivots = jnp.where(mine, pivot, pivots)
            row_left, row_right = row_left * reciprocal, row_right * reciprocal
            jordan_left = jnp.where(mine, row_left, jordan_left - column * row_left)
            jordan_right = jnp.where(mine, row_right, jordan_right - column * row_right)
            for m in range(l + 1, GROUP):
                row = down(columns[m], l) * reciprocal
                columns[m] = jnp.where(mine, row, columns[m] - column * row)
        inverse.append(forward_right * lax.rsqrt(pivots))
        rows_left = [down(jordan_left, l) for l in range(GROUP)]
        rows_right = [down(jordan_right, l) for l in range(GROUP)]
        for h in range(g + 1, groups):
            base = left[h]
            new_left, new_right = base, right[h]
            for l in range(GROUP):
                coefficient = across(base, first + l)
                new_left = new_left - coefficient * rows_left[l]
                new_right = new_right - coefficient * rows_right[l]
            left[h], right[h] = new_left, new_right
    return jnp.concatenate(inverse, axis=0)


def plain_factor_kernel(packed_ref, share_ref, ortho_ref, work):
    rank = work.shape[0]
    blocks = rank // BLOCK
    offset = 0
    for i in range(rank // PACK):
        for j in range(i + 1):
            tile = packed_ref[:, offset : offset + PACK]
            offset += PACK
            work[PACK * i : PACK * (i + 1), PACK * j : PACK * (j + 1)] = tile
            if j < i:
                work[PACK * j : PACK * (j + 1), PACK * i : PACK * (i + 1)] = tile.T
    column_block = lax.broadcasted_iota(jnp.int32, (BLOCK, rank), 1) // BLOCK

    def step(k, carry):
        here = pl.ds(pl.multiple_of(k * BLOCK, BLOCK), BLOCK)
        x = factor_block(work[here, here])
        pivot_rows = jnp.dot(x, work[here, :], precision=HIGHEST, preferred_element_type=jnp.float32)
        wide = jnp.concatenate([x] * blocks, axis=1)
        pivot_rows = jnp.where(column_block == k, wide, pivot_rows)
        work[here, :] = pivot_rows

        def below(i, carry):
            there = pl.ds(pl.multiple_of(i * BLOCK, BLOCK), BLOCK)
            panel = lax.dot_general(
                work[there, here], x, (((1,), (1,)), ((), ())),
                precision=HIGHEST, preferred_element_type=jnp.float32,
            )
            work[there, here] = jnp.zeros((BLOCK, BLOCK), jnp.float32)
            work[there, :] = work[there, :] - jnp.dot(
                panel, work[here, :], precision=HIGHEST, preferred_element_type=jnp.float32
            )
            return carry

        lax.fori_loop(k + 1, blocks, below, 0)
        rest = jnp.where(column_block <= k, pivot_rows, 0.0)
        total = jnp.zeros((share_ref.shape[0], BLOCK), jnp.float32)
        for _ in range(3):
            part = rest.astype(jnp.bfloat16)
            rest = rest - part.astype(jnp.float32)
            total = total + lax.dot_general(
                share_ref[...], part, (((1,), (1,)), ((), ())),
                preferred_element_type=jnp.float32,
            )
        ortho_ref[:, here] = total.astype(jnp.bfloat16)
        return carry

    lax.fori_loop(0, blocks, step, 0)


def orthonormalize(row_share, packed):
    rank = row_share.shape[1]
    return pl.pallas_call(
        plain_factor_kernel,
        out_shape=jax.ShapeDtypeStruct(row_share.shape, jnp.bfloat16),
        in_specs=[pl.BlockSpec(memory_space=pltpu.VMEM)] * 2,
        out_specs=pl.BlockSpec(memory_space=pltpu.VMEM),
        scratch_shapes=[pltpu.VMEM((rank, rank), jnp.float32)],
        compiler_params=pltpu.CompilerParams(vmem_limit_bytes=40 * 1024 * 1024),
        name="factor",
    )(packed, row_share)


def packed_gram(share):
    pieces = []
    for i in range(share.shape[1] // PACK):
        pieces.append(
            lax.dot_general(
                share[:, PACK * i : PACK * (i + 1)],
                share[:, : PACK * (i + 1)],
                (((0,), (0,)), ((), ())),
                preferred_element_type=jnp.float32,
            )
        )
    return jnp.concatenate(pieces, axis=1)


def plain_body(momentum, gradient, right_basis):
    buffer = (momentum.astype(jnp.float32) + gradient.astype(jnp.float32)).astype(jnp.bfloat16)
    rank_rows = right_basis.shape[0]
    partial_value = lax.dot_general(
        buffer,
        lax.all_gather(right_basis, "row", axis=0, tiled=True),
        (((1,), (1,)), ((), ())),
        preferred_element_type=jnp.float32,
    )
    row_share = lax.psum_scatter(
        partial_value.astype(jnp.bfloat16), "col", scatter_dimension=0, tiled=True
    )
    packed = lax.psum(packed_gram(row_share), ("row", "col"))
    ortho_share = orthonormalize(row_share, packed)
    orthonormal = lax.all_gather(ortho_share, "col", axis=0, tiled=True)
    right_share = lax.psum_scatter(
        lax.dot_general(
            orthonormal, buffer, (((0,), (0,)), ((), ())), preferred_element_type=jnp.float32
        ).astype(jnp.bfloat16),
        "row",
        scatter_dimension=0,
        tiled=True,
    )
    gathered = lax.all_gather(right_share, "row", axis=0, tiled=True)
    right_wide = right_share.astype(jnp.float32)
    sums = jnp.sum(right_wide * right_wide, axis=1)
    everyone = lax.all_gather(sums, ("row", "col"), axis=0)
    everyone = everyone.reshape(lax.axis_size("row"), lax.axis_size("col"), rank_rows)
    inverse_rows = lax.rsqrt(jnp.sum(everyone, axis=1) + epsilon)
    inverse_norm = inverse_rows.reshape(-1, 1)
    mine = lax.dynamic_index_in_dim(inverse_rows, lax.axis_index("row"), 0, keepdims=False)
    basis_next = right_wide * mine[:, None]
    scaled = (gathered.astype(jnp.float32) * inverse_norm).astype(jnp.bfloat16)
    feedback = jnp.dot(orthonormal, gathered, preferred_element_type=jnp.float32)
    direction = jnp.dot(orthonormal, scaled, preferred_element_type=jnp.float32)
    momentum_next = (buffer.astype(jnp.float32) - (1.0 - momentum_decay) * feedback).astype(
        jnp.bfloat16
    )
    update_scale = D / math.sqrt(RANK)
    update = (update_scale * direction).astype(jnp.bfloat16)
    return (momentum_next, basis_next, update)


MESH = pl.DeviceIdType.MESH
CHUNKS = 4
STACK = 9
F32 = jnp.float32
BF16 = jnp.bfloat16


def remote(src, dst, send_sem, recv_sem, device):
    return pltpu.make_async_remote_copy(
        src_ref=src, dst_ref=dst, send_sem=send_sem, recv_sem=recv_sem,
        device_id=device, device_id_type=MESH,
    )


def places():
    row, col = lax.axis_index("row"), lax.axis_index("col")
    return row, col, row // 2, lax.rem(row, 2), col // 2, lax.rem(col, 2)


def greet(devices):
    barrier = pltpu.get_barrier_semaphore()
    for device in devices:
        pl.semaphore_signal(barrier, inc=1, device_id=device, device_id_type=MESH)
    pl.semaphore_wait(barrier, len(devices))


def nt_dot(a, b):
    return lax.dot_general(a, b, (((1,), (1,)), ((), ())), preferred_element_type=F32)


def project_kernel(
    v_ref, m_hbm, g_hbm, pt_ref, b_hbm,
    buf, basis, m_tile, g_tile, part, core_in, half, y_in,
    load_sem, store_sem, own_send, hop_send, x_send, z_recv, x_recv,
    core_send, core_recv, y_send, y_recv, share_send, share_recv,
):
    row, col, z, x, y, k = places()
    rows = buf.shape[0]
    tile = m_tile.shape[1]
    tiles = rows // tile
    x_peer = (z * 2 + 1 - x, col)
    core_peer = (row, y * 2 + 1 - k)
    y_peer = (row, (1 - y) * 2 + k)
    middle = jnp.logical_and(z > 0, z < 3)
    order = [z, jnp.bitwise_xor(z, 1), jnp.where(z < 2, 2, 1), jnp.where(z < 2, 3, 0)]

    def load(i, slot):
        here = pl.ds(pl.multiple_of(i * tile, tile), tile)
        return (
            pltpu.make_async_copy(m_hbm.at[here], m_tile.at[slot], load_sem.at[0, slot]),
            pltpu.make_async_copy(g_hbm.at[here], g_tile.at[slot], load_sem.at[1, slot]),
        )

    for slot in range(2):
        for copy in load(slot, slot):
            copy.start()
    greet(
        [(lax.rem(z + 1, 4) * 2 + x, col), (lax.rem(z + 2, 4) * 2 + x, col), (lax.rem(z + 3, 4) * 2 + x, col)]
        + [x_peer, core_peer, y_peer]
    )
    own_up = remote(v_ref, basis.at[z, x], own_send.at[0], z_recv.at[z], (jnp.minimum(z + 1, 3) * 2 + x, col))
    own_down = remote(v_ref, basis.at[z, x], own_send.at[1], z_recv.at[z], (jnp.maximum(z - 1, 0) * 2 + x, col))
    own_side = remote(v_ref, basis.at[z, x], x_send.at[z], x_recv.at[z], x_peer)

    @pl.when(z < 3)
    def _():
        own_up.start()

    @pl.when(z > 0)
    def _():
        own_down.start()

    own_side.start()
    basis[z, x] = v_ref[...]

    def build(i, carry):
        slot = lax.rem(i, 2)
        for copy in load(i, slot):
            copy.wait()
        here = pl.ds(pl.multiple_of(i * tile, tile), tile)
        buf[here, :] = (m_tile[slot].astype(F32) + g_tile[slot].astype(F32)).astype(BF16)

        @pl.when(i + 2 < tiles)
        def _():
            for copy in load(i + 2, slot):
                copy.start()

        return carry

    lax.fori_loop(0, tiles, build, 0)
    store = pltpu.make_async_copy(buf, b_hbm, store_sem)
    store.start()

    def hop(s):
        q = order[s]
        target = jnp.where(z == 1, jnp.where(q < z, 2, 0), jnp.where(q < z, 3, 1))
        return remote(basis.at[q, x], basis.at[q, x], hop_send.at[s - 1], z_recv.at[q], (target * 2 + x, col))

    def side(s):
        q = order[s]
        return remote(basis.at[q, x], basis.at[q, x], x_send.at[q], x_recv.at[q], x_peer)

    def take(s):
        hop(s).wait_recv()

        @pl.when(middle)
        def _():
            hop(s).start()

        side(s).start()

    def side_in(s):
        q = order[s]
        remote(basis.at[q, x], basis.at[q, 1 - x], x_send.at[q], x_recv.at[q], x_peer).wait_recv()

    wide = rows // 2

    def to_core(s, h):
        here = pl.ds(h * wide, wide)
        return remote(
            part.at[s, 1 - k, :, here], core_in.at[s, :, here], core_send.at[s, h], core_recv.at[s, h], core_peer
        )

    def to_y(s, h):
        here = pl.ds(h * wide, wide)
        return remote(half.at[s, :, here], y_in.at[s, :, here], y_send.at[s, h], y_recv.at[s, h], y_peer)

    def share(s, h):
        here = pl.ds(h * wide, wide)
        spot = pt_ref.at[order[s], k, :, here]
        return remote(spot, spot, share_send.at[s, h], share_recv.at[s, h], core_peer)

    def share_in(s, h):
        here = pl.ds(h * wide, wide)
        return remote(
            pt_ref.at[order[s], k, :, here], pt_ref.at[order[s], 1 - k, :, here],
            share_send.at[s, h], share_recv.at[s, h], core_peer,
        )

    def multiply(s):
        q = order[s]
        width = 512
        for h in range(2):

            def columns(n, carry):
                here = pl.ds(pl.multiple_of(n * width, width), width)
                left = basis[q].reshape(2 * basis.shape[2], basis.shape[3])
                value = nt_dot(left, buf[here, :])
                part[s, :, :, here] = value.astype(BF16).reshape(2, basis.shape[2], width)
                return carry

            lax.fori_loop(h * (wide // width), (h + 1) * (wide // width), columns, 0)
            to_core(s, h).start()

    def add_core(s):
        for h in range(2):
            here = slice(h * wide, (h + 1) * wide)
            to_core(s, h).wait_recv()
            half[s, :, here] = (part[s, k, :, here].astype(F32) + core_in[s, :, here].astype(F32)).astype(BF16)
            to_y(s, h).start()

    def add_y(s):
        for h in range(2):
            here = slice(h * wide, (h + 1) * wide)
            to_y(s, h).wait_recv()
            pt_ref[order[s], k, :, here] = (half[s, :, here].astype(F32) + y_in[s, :, here].astype(F32)).astype(BF16)
            share(s, h).start()

    take(1)

    @pl.when(middle)
    def _():
        take(2)

    side_in(0)
    multiply(0)

    @pl.when(jnp.logical_not(middle))
    def _():
        take(2)

    add_core(0)

    @pl.when(middle)
    def _():
        take(3)

    side_in(1)
    multiply(1)
    add_y(0)
    add_core(1)

    @pl.when(jnp.logical_not(middle))
    def _():
        take(3)

    side_in(2)
    multiply(2)
    add_y(1)
    add_core(2)
    side_in(3)
    multiply(3)
    add_y(2)
    add_core(3)
    add_y(3)

    @pl.when(z < 3)
    def _():
        own_up.wait_send()

    @pl.when(z > 0)
    def _():
        own_down.wait_send()

    own_side.wait_send()

    @pl.when(middle)
    def _():
        for s in range(1, 4):
            hop(s).wait_send()

    for s in range(1, 4):
        side(s).wait_send()
    for s in range(4):
        for h in range(2):
            to_core(s, h).wait_send()
            to_y(s, h).wait_send()
            share(s, h).wait_send()
            share_in(s, h).wait_recv()
    store.wait()


def project(v, m, g):
    rows, columns = m.shape
    ranks = v.shape[0]
    dma = pltpu.SemaphoreType.DMA
    vmem = pl.BlockSpec(memory_space=pltpu.VMEM)
    anywhere = pl.BlockSpec(memory_space=pl.ANY)
    return pl.pallas_call(
        project_kernel,
        out_shape=(
            jax.ShapeDtypeStruct((4, 2, ranks, rows), BF16),
            jax.ShapeDtypeStruct((rows, columns), BF16),
        ),
        in_specs=[vmem, anywhere, anywhere],
        out_specs=(vmem, anywhere),
        scratch_shapes=[
            pltpu.VMEM((rows, columns), BF16),
            pltpu.VMEM((4, 2, ranks, columns), BF16),
            pltpu.VMEM((2, 128, columns), BF16),
            pltpu.VMEM((2, 128, columns), BF16),
            pltpu.VMEM((4, 2, ranks, rows), BF16),
            pltpu.VMEM((4, ranks, rows), BF16),
            pltpu.VMEM((4, ranks, rows), BF16),
            pltpu.VMEM((4, ranks, rows), BF16),
            dma((2, 2)), dma, dma((2,)), dma((3,)), dma((4,)), dma((4,)), dma((4,)),
            dma((4, 2)), dma((4, 2)), dma((4, 2)), dma((4, 2)), dma((4, 2)), dma((4, 2)),
        ],
        compiler_params=pltpu.CompilerParams(
            collective_id=1, has_side_effects=True, vmem_limit_bytes=58 * 1024 * 1024
        ),
        cost_estimate=pl.CostEstimate(flops=2 * rows * columns * ranks * 8, bytes_accessed=6 * rows * columns, transcendentals=0),
        name="project",
    )(v, m, g)


def factor_kernel(
    pt_ref, b_hbm, o_ref, n_hbm, m_hbm, sums_ref,
    buf, wpart, x_in, z_in, whole, stack, stack_in, stack_all, work, inverse, squares, norm_in,
    load_sem, store_sem, back_sem, xs, xr, zs, zr, gs, gr, fs, ys,
    ss, sr, ts, tr, us, ur, ns, nr,
):
    row, col, z, x, y, k = places()
    ranks = pt_ref.shape[2]
    rank = work.shape[0]
    blocks = rank // BLOCK
    chunks = wpart.shape[0]
    width = wpart.shape[4]
    slice_rows = stack_in.shape[1]
    x_peer = (z * 2 + 1 - x, col)
    core_peer = (row, y * 2 + 1 - k)
    y_peer = (row, (1 - y) * 2 + k)

    def z_of(shift):
        return lax.rem(z + shift, 4)

    def z_peer(shift):
        return (z_of(shift) * 2 + x, col)

    def row_of(shift):
        return lax.rem(row + shift, 8)

    def load(j):
        return pltpu.make_async_copy(
            b_hbm.at[:, pl.ds(j * width, width)], buf.at[j % 2], load_sem.at[j % 2]
        )

    load(0).start()
    load(1).start()
    greet([(row_of(shift), col) for shift in range(1, 8)] + [core_peer, y_peer])

    def gram(t, carry):
        early = t < 8 - col
        i = jnp.where(early, col + t, t - 1)
        j = jnp.where(early, col, 7 - col)
        value = nt_dot(pt_ref[i // 2, lax.rem(i, 2)], pt_ref[j // 2, lax.rem(j, 2)])
        stack[pl.ds(pl.multiple_of(t * BLOCK, BLOCK), BLOCK), :] = value
        return carry

    lax.fori_loop(0, STACK, gram, 0)

    def part_of(r):
        return pl.ds(pl.multiple_of(r * slice_rows, slice_rows), slice_rows)

    def gram_out(shift):
        to = row_of(shift)
        return remote(stack.at[part_of(to)], stack_in.at[row], ss.at[shift], sr.at[row], (to, col))

    def gram_in(shift):
        who = row_of(shift)
        return remote(stack.at[part_of(row)], stack_in.at[who], ss.at[shift], sr.at[who], (who, col))

    def sum_out(shift):
        to = row_of(shift)
        return remote(stack_all.at[col, part_of(row)], stack_all.at[col, part_of(row)], ts.at[shift], tr.at[row], (to, col))

    def sum_in(shift):
        who = row_of(shift)
        return remote(stack_all.at[col, part_of(who)], stack_all.at[col, part_of(who)], ts.at[shift], tr.at[who], (who, col))

    def spread(index, what, device):
        return remote(stack_all.at[what], stack_all.at[what], us.at[index], ur.at[index], device)

    for shift in range(1, 8):
        gram_out(shift).start()

    def side_out(j):
        return remote(wpart.at[j, :, 1 - x], x_in.at[j], xs.at[j], xr.at[j], x_peer)

    def weigh(j, which):
        step = 256

        def columns(n, carry):
            here = pl.ds(pl.multiple_of(n * step, step), step)
            left = pt_ref[:, which].reshape(4 * ranks, pt_ref.shape[3])
            value = jnp.dot(left, buf[j % 2, :, here], preferred_element_type=F32)
            wpart[j, :, which, :, here] = value.astype(BF16).reshape(4, ranks, step)
            return carry

        lax.fori_loop(0, width // step, columns, 0)

    def product(j):
        load(j).wait()
        weigh(j, 1 - x)
        if j < 1:
            side_out(j).start()
        weigh(j, x)
        if j + 2 < chunks:
            load(j + 2).start()

    end = jnp.logical_or(z == 0, z == 3)
    low = z < 2

    def line_send(j, i, piece, to, slot):
        return remote(x_in.at[j, piece], z_in.at[j, slot], zs.at[j, i], zr.at[j, slot], (to * 2 + x, col))

    def line_take(j, slot):
        remote(x_in.at[j, 0], z_in.at[j, slot], zs.at[j, 0], zr.at[j, slot], x_peer).wait_recv()

    def line_first(j):
        for i in range(3):
            piece = jnp.where(low, 3 - i, i)
            slot = piece if i < 2 else jnp.where(low, 1, 4)
            line_send(j, i, piece, jnp.where(low, 1, 2), slot).start()

    def add_in(j, piece):
        line_take(j, piece)
        x_in[j, piece] = (x_in[j, piece].astype(F32) + z_in[j, piece].astype(F32)).astype(BF16)

    def add_side(j):
        side_out(j).wait_recv()
        if j + 1 < chunks:
            side_out(j + 1).start()
        for shift in (1, 2, 3, 0):
            there = z_of(shift)
            x_in[j, there] = (wpart[j, there, x].astype(F32) + x_in[j, there].astype(F32)).astype(BF16)

        @pl.when(end)
        def _():
            line_first(j)

    def line_second(j):
        @pl.when(jnp.logical_not(end))
        def _():
            for i in range(2):
                piece = jnp.where(low, 3 - i, i)
                slot = piece if i < 1 else jnp.where(low, 2, 4)
                add_in(j, piece)
                line_send(j, i, piece, jnp.where(low, 2, 1), slot).start()

    def line_third(j):
        @pl.when(jnp.logical_not(end))
        def _():
            piece = jnp.where(low, 0, 3)
            add_in(j, piece)
            line_send(j, 2, piece, piece, jnp.where(low, 4, 3)).start()

    order = [z, jnp.bitwise_xor(z, 1), jnp.where(low, 2, 1), jnp.where(low, 3, 0)]

    def full_send(j, q, sem, to):
        return remote(whole.at[j, q, x], whole.at[j, q, x], gs.at[j, sem], gr.at[j, q], (to * 2 + x, col))

    def own_up(j):
        return full_send(j, z, 0, jnp.minimum(z + 1, 3))

    def own_down(j):
        return full_send(j, z, 1, jnp.maximum(z - 1, 0))

    def hop(j, s):
        q = order[s]
        return full_send(j, q, s + 1, jnp.where(low, jnp.where(q < z, 2, 0), jnp.where(q < z, 3, 1)))

    def full_side(j, q):
        return remote(whole.at[j, q, x], whole.at[j, q, x], fs.at[j, q], ys.at[j, q], x_peer)

    def full_side_in(j, q):
        return remote(whole.at[j, q, x], whole.at[j, q, 1 - x], fs.at[j, q], ys.at[j, q], x_peer)

    def finish(j):
        @pl.when(z > 0)
        def _():
            line_take(j, z)
            x_in[j, z] = (x_in[j, z].astype(F32) + z_in[j, z].astype(F32)).astype(BF16)

        @pl.when(z < 3)
        def _():
            line_take(j, 4)
            x_in[j, z] = (x_in[j, z].astype(F32) + z_in[j, 4].astype(F32)).astype(BF16)

        whole[j, z, x] = x_in[j, z]

        @pl.when(z < 3)
        def _():
            own_up(j).start()

        @pl.when(z > 0)
        def _():
            own_down(j).start()

        full_side(j, z).start()

    def take(j, s):
        hop(j, s).wait_recv()

        @pl.when(jnp.logical_not(end))
        def _():
            hop(j, s).start()

        full_side(j, order[s]).start()

    def take_first(j):
        take(j, 1)

        @pl.when(jnp.logical_not(end))
        def _():
            take(j, 2)

    def take_second(j):
        @pl.when(end)
        def _():
            take(j, 2)

    def take_third(j):
        take(j, 3)

    def sum_gram():
        total = stack[part_of(row), :]
        for shift in range(1, 8):
            gram_in(shift).wait_recv()
            total = total + stack_in[row_of(shift)]
        stack_all[col, part_of(row), :] = total
        for shift in range(1, 8):
            sum_out(shift).start()

    other_col = (1 - y) * 2 + k

    def spread_gram():
        for shift in range(1, 8):
            sum_in(shift).wait_recv()
        spread(1, col, y_peer).start()
        spread(0, col, core_peer).start()

    def end_gram():
        spread(1, other_col, y_peer).wait_recv()
        spread(2, other_col, core_peer).start()
        spread(0, y * 2 + 1 - k, core_peer).wait_recv()
        spread(2, (1 - y) * 2 + 1 - k, core_peer).wait_recv()

    product(0)
    product(1)
    product(2)
    product(3)
    sum_gram()
    add_side(0)
    spread_gram()
    line_second(0)
    end_gram()

    for c in range(4):
        for t in range(STACK):
            i, j = (c + t, c) if t < 8 - c else (t - 1, 7 - c)
            value = stack_all[c, BLOCK * t : BLOCK * (t + 1), :]
            work[BLOCK * i : BLOCK * (i + 1), BLOCK * j : BLOCK * (j + 1)] = value
            if i != j:
                work[BLOCK * j : BLOCK * (j + 1), BLOCK * i : BLOCK * (i + 1)] = value.T

    column_block = lax.broadcasted_iota(jnp.int32, (BLOCK, rank), 1) // BLOCK
    events = {
        0: [(add_side, 1), (line_third, 0)],
        1: [(finish, 0), (line_second, 1)],
        2: [(add_side, 2), (line_third, 1)],
        3: [(take_first, 0), (finish, 1)],
        4: [(line_second, 2), (take_second, 0)],
        5: [(add_side, 3), (line_third, 2), (take_third, 0), (take_first, 1)],
        6: [(finish, 2), (line_second, 3)],
        7: [(take_second, 1), (line_third, 3), (take_third, 1)],
    }

    def step(kk, carry):
        here = pl.ds(pl.multiple_of(kk * BLOCK, BLOCK), BLOCK)
        factor = factor_block(work[here, here])
        pivot_rows = jnp.dot(factor, work[here, :], precision=HIGHEST, preferred_element_type=F32)
        wide = jnp.concatenate([factor] * blocks, axis=1)
        pivot_rows = jnp.where(column_block == kk, wide, pivot_rows)
        work[here, :] = pivot_rows

        def below(i, carry):
            there = pl.ds(pl.multiple_of(i * BLOCK, BLOCK), BLOCK)
            panel = lax.dot_general(
                work[there, here], factor, (((1,), (1,)), ((), ())),
                precision=HIGHEST, preferred_element_type=F32,
            )
            work[there, here] = jnp.zeros((BLOCK, BLOCK), F32)
            work[there, :] = work[there, :] - jnp.dot(
                panel, work[here, :], precision=HIGHEST, preferred_element_type=F32
            )
            return carry

        lax.fori_loop(kk + 1, blocks, below, 0)
        rest = jnp.where(column_block <= kk, pivot_rows, 0.0)
        high = rest.astype(BF16)
        inverse[0, here, :] = high
        inverse[1, here, :] = (rest - high.astype(F32)).astype(BF16)
        for at, todo in events.items():
            if todo:
                @pl.when(kk == at)
                def _(todo=todo):
                    for function, j in todo:
                        function(j)
        return carry

    lax.fori_loop(0, blocks, step, 0)

    def apply(load_right, store_out, columns):
        tile = 512

        def one(n, carry):
            here = pl.ds(pl.multiple_of(n * tile, tile), tile)
            right = load_right(here)
            for i in range(4):
                rows = slice(256 * i, 256 * (i + 1))
                deep = 256 * (i + 1)
                left = inverse[:, rows, :deep].reshape(512, deep)
                value = jnp.dot(left, right[:deep], preferred_element_type=F32)
                store_out(i, here, value[:256] + value[256:])
            return carry

        lax.fori_loop(0, columns // tile, one, 0)

    def p_load(here):
        return pt_ref[:, :, :, here].reshape(rank, 512)

    def o_store(i, here, value):
        o_ref[here, 256 * i : 256 * (i + 1)] = value.T.astype(BF16)

    load(0).start()
    load(1).start()
    finish(3)
    take_first(2)
    apply(p_load, o_store, pt_ref.shape[3])
    squares[...] = jnp.zeros_like(squares)

    def store(j):
        return pltpu.make_async_copy(
            wpart.at[j], n_hbm.at[:, :, :, pl.ds(j * width, width)], store_sem.at[j]
        )

    def back(j):
        return pltpu.make_async_copy(
            buf.at[j % 2], m_hbm.at[:, pl.ds(j * width, width)], back_sem.at[j % 2]
        )

    def right(j):
        for q in range(4):
            full_side_in(j, q).wait_recv()
        side_out(j).wait_send()

        def w_load(here):
            return whole[j, :, :, :, here].reshape(rank, 512)

        def n_store(i, here, value):
            low = value.astype(BF16)
            wpart[j, i, :, :, here] = low.reshape(2, ranks, 512)
            low = low.astype(F32)
            low = low * low
            squares[256 * i : 256 * (i + 1), :] += sum(
                low[:, BLOCK * g : BLOCK * (g + 1)] for g in range(1, 4)
            ) + low[:, :BLOCK]

        apply(w_load, n_store, width)
        store(j).start()

    def feed_back(j):
        load(j).wait()
        tall, wide = 512, 512

        def one(t, carry):
            across_tiles = width // wide
            rows = pl.ds(pl.multiple_of(t // across_tiles * tall, tall), tall)
            here = pl.ds(pl.multiple_of(lax.rem(t, across_tiles) * wide, wide), wide)
            value = jnp.dot(
                o_ref[rows, :], wpart[j, :, :, :, here].reshape(rank, wide), preferred_element_type=F32
            )
            old = buf[j % 2, rows, here].astype(F32)
            buf[j % 2, rows, here] = (old - (1.0 - momentum_decay) * value).astype(BF16)
            return carry

        lax.fori_loop(0, buf.shape[1] // tall * (width // wide), one, 0)
        back(j).start()
        if j + 2 < chunks:
            back(j).wait()
            load(j + 2).start()

    take_second(2)
    right(0)
    take_third(2)
    take_first(3)
    feed_back(0)
    take_second(3)
    right(1)
    take_third(3)
    feed_back(1)
    right(2)
    feed_back(2)
    right(3)

    def norm(shift):
        to = lax.rem(col + shift, 4)
        return remote(norm_in.at[col], norm_in.at[col], ns.at[shift], nr.at[col], (row, to))

    def norm_from(shift):
        who = lax.rem(col + shift, 4)
        return remote(norm_in.at[who], norm_in.at[who], ns.at[shift], nr.at[who], (row, who))

    ones = jnp.ones((GROUP, BLOCK), F32)
    norm_in[col] = lax.dot_general(
        ones, squares[...], (((1,), (1,)), ((), ())), precision=HIGHEST, preferred_element_type=F32
    )
    for shift in range(1, 4):
        norm(shift).start()
    feed_back(3)
    for shift in range(1, 4):
        norm_from(shift).wait_recv()
    sums_ref[...] = (norm_in[0] + norm_in[1]) + (norm_in[2] + norm_in[3])
    for shift in range(1, 4):
        norm(shift).wait_send()
    for shift in range(1, 8):
        gram_out(shift).wait_send()
        sum_out(shift).wait_send()
    spread(0, col, core_peer).wait_send()
    spread(1, col, y_peer).wait_send()
    spread(2, other_col, core_peer).wait_send()
    for j in range(chunks):
        for i in range(3):
            line_send(j, i, 0, z, 0).wait_send()

        @pl.when(z < 3)
        def _():
            own_up(j).wait_send()

        @pl.when(z > 0)
        def _():
            own_down(j).wait_send()

        @pl.when(jnp.logical_not(end))
        def _():
            for s in range(1, 4):
                hop(j, s).wait_send()

        for q in range(4):
            full_side(j, q).wait_send()
        store(j).wait()
    back(chunks - 2).wait()
    back(chunks - 1).wait()


def factorize(pt, b):
    _, _, ranks, rows = pt.shape
    columns = b.shape[1]
    rank = 8 * ranks
    width = columns // CHUNKS
    slice_rows = STACK * BLOCK // 8
    dma = pltpu.SemaphoreType.DMA
    vmem = pl.BlockSpec(memory_space=pltpu.VMEM)
    anywhere = pl.BlockSpec(memory_space=pl.ANY)
    return pl.pallas_call(
        factor_kernel,
        out_shape=(
            jax.ShapeDtypeStruct((rows, rank), BF16),
            jax.ShapeDtypeStruct((4, 2, ranks, columns), BF16),
            jax.ShapeDtypeStruct((rows, columns), BF16),
            jax.ShapeDtypeStruct((GROUP, rank), F32),
        ),
        in_specs=[vmem, anywhere],
        out_specs=(vmem, anywhere, anywhere, vmem),
        scratch_shapes=[
            pltpu.VMEM((2, rows, width), BF16),
            pltpu.VMEM((CHUNKS, 4, 2, ranks, width), BF16),
            pltpu.VMEM((CHUNKS, 4, ranks, width), BF16),
            pltpu.VMEM((CHUNKS, 5, ranks, width), BF16),
            pltpu.VMEM((CHUNKS, 4, 2, ranks, width), BF16),
            pltpu.VMEM((STACK * BLOCK, BLOCK), F32),
            pltpu.VMEM((8, slice_rows, BLOCK), F32),
            pltpu.VMEM((4, STACK * BLOCK, BLOCK), F32),
            pltpu.VMEM((rank, rank), F32),
            pltpu.VMEM((2, rank, rank), BF16),
            pltpu.VMEM((rank, BLOCK), F32),
            pltpu.VMEM((4, GROUP, rank), F32),
            dma((2,)), dma((CHUNKS,)), dma((2,)), dma((CHUNKS,)), dma((CHUNKS,)),
            dma((CHUNKS, 3)), dma((CHUNKS, 5)), dma((CHUNKS, 5)), dma((CHUNKS, 4)),
            dma((CHUNKS, 4)), dma((CHUNKS, 4)),
            dma((8,)), dma((8,)), dma((8,)), dma((8,)), dma((3,)), dma((3,)), dma((4,)), dma((4,)),
        ],
        compiler_params=pltpu.CompilerParams(
            collective_id=2, has_side_effects=True, vmem_limit_bytes=58 * 1024 * 1024
        ),
        name="factorize",
    )(pt, b)


def update_kernel(o_ref, n_ref, m_ref, sums_ref, m_out, basis_ref, update_ref, inverse, left):
    ranks = basis_ref.shape[0]
    rows = o_ref.shape[0]
    pieces = 4
    tall = rows // pieces

    @pl.when(pl.program_id(0) == 0)
    def _():
        norm = lax.rsqrt(sums_ref[0:1, :] + epsilon)
        inverse[...] = jnp.broadcast_to(norm, (BLOCK, norm.shape[1])).T
        scale = D / math.sqrt(RANK) * norm
        for i in range(pieces):
            part = slice(i * tall, (i + 1) * tall)
            left[part, :] = (o_ref[part, :].astype(F32) * scale).astype(BF16)

    width = n_ref.shape[1]
    mine = pl.ds(pl.multiple_of(lax.axis_index("row") * ranks, ranks), ranks)
    own = jnp.concatenate([inverse[mine, :]] * (width // BLOCK), axis=1)
    basis_ref[...] = n_ref[mine, :].astype(F32) * own
    for i in range(pieces):
        part = slice(i * tall, (i + 1) * tall)
        update_ref[part, :] = jnp.dot(
            left[part, :], n_ref[...], preferred_element_type=F32
        ).astype(BF16)
        m_out[part, :] = m_ref[part, :]


def finish_update(ortho, right_new, momentum_next, sums, ranks):
    rows, columns = momentum_next.shape
    rank = ortho.shape[1]
    width = 512

    def strip(height):
        return pl.BlockSpec((height, width), lambda j: (0, j))

    def fixed(shape):
        return pl.BlockSpec(shape, lambda j: (0, 0))

    return pl.pallas_call(
        update_kernel,
        grid=(columns // width,),
        out_shape=(
            jax.ShapeDtypeStruct((rows, columns), BF16),
            jax.ShapeDtypeStruct((ranks, columns), F32),
            jax.ShapeDtypeStruct((rows, columns), BF16),
        ),
        in_specs=[fixed((rows, rank)), strip(rank), strip(rows), fixed((GROUP, rank))],
        out_specs=(strip(rows), strip(ranks), strip(rows)),
        scratch_shapes=[
            pltpu.VMEM((rank, BLOCK), F32),
            pltpu.VMEM((rows, rank), BF16),
        ],
        compiler_params=pltpu.CompilerParams(vmem_limit_bytes=58 * 1024 * 1024),
        cost_estimate=pl.CostEstimate(flops=2 * rows * columns * rank, bytes_accessed=8 * rows * columns, transcendentals=0),
        name="update",
    )(ortho, right_new, momentum_next, sums)


def body(momentum, gradient, right_basis):
    pt, buffer = project(right_basis, momentum, gradient)
    ortho, right_new, momentum_next, sums = factorize(pt, buffer)
    right_new = right_new.reshape(ortho.shape[1], buffer.shape[1])
    return finish_update(ortho, right_new, momentum_next, sums, right_basis.shape[0])


def solution(mesh):
    sizes = (mesh.shape["row"], mesh.shape["col"])
    return jax.shard_map(
        body if sizes == (8, 4) else plain_body,
        mesh=mesh,
        in_specs=(P("row", "col"), P("row", "col"), P("row", "col")),
        out_specs=(P("row", "col"), P("row", "col"), P("row", "col")),
        check_vma=False,
    )
```

```python
import functools
import math

import jax
import jax.numpy as jnp
from jax import lax
from jax.experimental import pallas as pl
from jax.experimental.pallas import tpu as pltpu
from jax.sharding import PartitionSpec as P

D = 16384
RANK = 1024

momentum_decay = 0.95
epsilon = 1e-06

BLOCK = 128
GROUP = 8
PACK = 256

HIGHEST = lax.Precision.HIGHEST


def across(x, column):
    return jnp.broadcast_to(x[:, column : column + 1], (x.shape[0], BLOCK))


def down(x, row):
    return jnp.broadcast_to(x[row : row + 1, :], (GROUP, BLOCK))


def factor_block(block):
    groups = BLOCK // GROUP
    sub = lax.broadcasted_iota(jnp.int32, (GROUP, BLOCK), 0)
    lane = lax.broadcasted_iota(jnp.int32, (GROUP, BLOCK), 1)
    left = [block[GROUP * g : GROUP * (g + 1), :] for g in range(groups)]
    right = [jnp.where(lane == sub + GROUP * g, 1.0, 0.0) for g in range(groups)]
    inverse = []
    for g in range(groups):
        first = GROUP * g
        jordan_left, jordan_right = left[g], right[g]
        columns = [across(jordan_left, first + l) for l in range(GROUP)]
        forward_right, pivots = jordan_right, jnp.ones_like(jordan_left)
        for l in range(GROUP):
            pivot = down(columns[l], l)
            reciprocal = 1.0 / pivot
            mine = sub == l
            column = columns[l]
            row_left, row_right = down(jordan_left, l), down(jordan_right, l)
            forward_right = jnp.where(mine, row_right, forward_right)
            pivots = jnp.where(mine, pivot, pivots)
            row_left, row_right = row_left * reciprocal, row_right * reciprocal
            jordan_left = jnp.where(mine, row_left, jordan_left - column * row_left)
            jordan_right = jnp.where(mine, row_right, jordan_right - column * row_right)
            for m in range(l + 1, GROUP):
                row = down(columns[m], l) * reciprocal
                columns[m] = jnp.where(mine, row, columns[m] - column * row)
        inverse.append(forward_right * lax.rsqrt(pivots))
        rows_left = [down(jordan_left, l) for l in range(GROUP)]
        rows_right = [down(jordan_right, l) for l in range(GROUP)]
        for h in range(g + 1, groups):
            base = left[h]
            new_left, new_right = base, right[h]
            for l in range(GROUP):
                coefficient = across(base, first + l)
                new_left = new_left - coefficient * rows_left[l]
                new_right = new_right - coefficient * rows_right[l]
            left[h], right[h] = new_left, new_right
    return jnp.concatenate(inverse, axis=0)


def plain_factor_kernel(packed_ref, share_ref, ortho_ref, work):
    rank = work.shape[0]
    blocks = rank // BLOCK
    offset = 0
    for i in range(rank // PACK):
        for j in range(i + 1):
            tile = packed_ref[:, offset : offset + PACK]
            offset += PACK
            work[PACK * i : PACK * (i + 1), PACK * j : PACK * (j + 1)] = tile
            if j < i:
                work[PACK * j : PACK * (j + 1), PACK * i : PACK * (i + 1)] = tile.T
    column_block = lax.broadcasted_iota(jnp.int32, (BLOCK, rank), 1) // BLOCK

    def step(k, carry):
        here = pl.ds(pl.multiple_of(k * BLOCK, BLOCK), BLOCK)
        x = factor_block(work[here, here])
        pivot_rows = jnp.dot(x, work[here, :], precision=HIGHEST, preferred_element_type=jnp.float32)
        wide = jnp.concatenate([x] * blocks, axis=1)
        pivot_rows = jnp.where(column_block == k, wide, pivot_rows)
        work[here, :] = pivot_rows

        def below(i, carry):
            there = pl.ds(pl.multiple_of(i * BLOCK, BLOCK), BLOCK)
            panel = lax.dot_general(
                work[there, here], x, (((1,), (1,)), ((), ())),
                precision=HIGHEST, preferred_element_type=jnp.float32,
            )
            work[there, here] = jnp.zeros((BLOCK, BLOCK), jnp.float32)
            work[there, :] = work[there, :] - jnp.dot(
                panel, work[here, :], precision=HIGHEST, preferred_element_type=jnp.float32
            )
            return carry

        lax.fori_loop(k + 1, blocks, below, 0)
        rest = jnp.where(column_block <= k, pivot_rows, 0.0)
        total = jnp.zeros((share_ref.shape[0], BLOCK), jnp.float32)
        for _ in range(3):
            part = rest.astype(jnp.bfloat16)
            rest = rest - part.astype(jnp.float32)
            total = total + lax.dot_general(
                share_ref[...], part, (((1,), (1,)), ((), ())),
                preferred_element_type=jnp.float32,
            )
        ortho_ref[:, here] = total.astype(jnp.bfloat16)
        return carry

    lax.fori_loop(0, blocks, step, 0)


def orthonormalize(row_share, packed):
    rank = row_share.shape[1]
    return pl.pallas_call(
        plain_factor_kernel,
        out_shape=jax.ShapeDtypeStruct(row_share.shape, jnp.bfloat16),
        in_specs=[pl.BlockSpec(memory_space=pltpu.VMEM)] * 2,
        out_specs=pl.BlockSpec(memory_space=pltpu.VMEM),
        scratch_shapes=[pltpu.VMEM((rank, rank), jnp.float32)],
        compiler_params=pltpu.CompilerParams(vmem_limit_bytes=40 * 1024 * 1024),
        name="factor",
    )(packed, row_share)


def packed_gram(share):
    pieces = []
    for i in range(share.shape[1] // PACK):
        pieces.append(
            lax.dot_general(
                share[:, PACK * i : PACK * (i + 1)],
                share[:, : PACK * (i + 1)],
                (((0,), (0,)), ((), ())),
                preferred_element_type=jnp.float32,
            )
        )
    return jnp.concatenate(pieces, axis=1)


def plain_body(momentum, gradient, right_basis):
    buffer = (momentum.astype(jnp.float32) + gradient.astype(jnp.float32)).astype(jnp.bfloat16)
    rank_rows = right_basis.shape[0]
    partial_value = lax.dot_general(
        buffer,
        lax.all_gather(right_basis, "row", axis=0, tiled=True),
        (((1,), (1,)), ((), ())),
        preferred_element_type=jnp.float32,
    )
    row_share = lax.psum_scatter(
        partial_value.astype(jnp.bfloat16), "col", scatter_dimension=0, tiled=True
    )
    packed = lax.psum(packed_gram(row_share), ("row", "col"))
    ortho_share = orthonormalize(row_share, packed)
    orthonormal = lax.all_gather(ortho_share, "col", axis=0, tiled=True)
    right_share = lax.psum_scatter(
        lax.dot_general(
            orthonormal, buffer, (((0,), (0,)), ((), ())), preferred_element_type=jnp.float32
        ).astype(jnp.bfloat16),
        "row",
        scatter_dimension=0,
        tiled=True,
    )
    gathered = lax.all_gather(right_share, "row", axis=0, tiled=True)
    right_wide = right_share.astype(jnp.float32)
    sums = jnp.sum(right_wide * right_wide, axis=1)
    everyone = lax.all_gather(sums, ("row", "col"), axis=0)
    everyone = everyone.reshape(lax.axis_size("row"), lax.axis_size("col"), rank_rows)
    inverse_rows = lax.rsqrt(jnp.sum(everyone, axis=1) + epsilon)
    inverse_norm = inverse_rows.reshape(-1, 1)
    mine = lax.dynamic_index_in_dim(inverse_rows, lax.axis_index("row"), 0, keepdims=False)
    basis_next = right_wide * mine[:, None]
    scaled = (gathered.astype(jnp.float32) * inverse_norm).astype(jnp.bfloat16)
    feedback = jnp.dot(orthonormal, gathered, preferred_element_type=jnp.float32)
    direction = jnp.dot(orthonormal, scaled, preferred_element_type=jnp.float32)
    momentum_next = (buffer.astype(jnp.float32) - (1.0 - momentum_decay) * feedback).astype(
        jnp.bfloat16
    )
    update_scale = D / math.sqrt(RANK)
    update = (update_scale * direction).astype(jnp.bfloat16)
    return (momentum_next, basis_next, update)


MESH = pl.DeviceIdType.MESH
CHUNKS = 4
STACK = 9
F32 = jnp.float32
BF16 = jnp.bfloat16


def remote(src, dst, send_sem, recv_sem, device):
    return pltpu.make_async_remote_copy(
        src_ref=src, dst_ref=dst, send_sem=send_sem, recv_sem=recv_sem,
        device_id=device, device_id_type=MESH,
    )


def places():
    row, col = lax.axis_index("row"), lax.axis_index("col")
    return row, col, row // 2, lax.rem(row, 2), col // 2, lax.rem(col, 2)


def greet(devices):
    barrier = pltpu.get_barrier_semaphore()
    for device in devices:
        pl.semaphore_signal(barrier, inc=1, device_id=device, device_id_type=MESH)
    pl.semaphore_wait(barrier, len(devices))


def nt_dot(a, b):
    return lax.dot_general(a, b, (((1,), (1,)), ((), ())), preferred_element_type=F32)


def project_kernel(
    v_ref, m_hbm, g_hbm, pt_ref, b_hbm,
    buf, basis, m_tile, g_tile, part, core_in, half, y_in,
    load_sem, store_sem, own_send, hop_send, x_send, z_recv, x_recv,
    core_send, core_recv, y_send, y_recv, share_send, share_recv,
):
    row, col, z, x, y, k = places()
    rows = buf.shape[0]
    tile = m_tile.shape[1]
    tiles = rows // tile
    x_peer = (z * 2 + 1 - x, col)
    core_peer = (row, y * 2 + 1 - k)
    y_peer = (row, (1 - y) * 2 + k)
    middle = jnp.logical_and(z > 0, z < 3)
    order = [z, jnp.bitwise_xor(z, 1), jnp.where(z < 2, 2, 1), jnp.where(z < 2, 3, 0)]

    def load(i, slot):
        here = pl.ds(pl.multiple_of(i * tile, tile), tile)
        return (
            pltpu.make_async_copy(m_hbm.at[here], m_tile.at[slot], load_sem.at[0, slot]),
            pltpu.make_async_copy(g_hbm.at[here], g_tile.at[slot], load_sem.at[1, slot]),
        )

    for slot in range(2):
        for copy in load(slot, slot):
            copy.start()
    greet(
        [(lax.rem(z + 1, 4) * 2 + x, col), (lax.rem(z + 2, 4) * 2 + x, col), (lax.rem(z + 3, 4) * 2 + x, col)]
        + [x_peer, core_peer, y_peer]
    )
    own_up = remote(v_ref, basis.at[z, x], own_send.at[0], z_recv.at[z], (jnp.minimum(z + 1, 3) * 2 + x, col))
    own_down = remote(v_ref, basis.at[z, x], own_send.at[1], z_recv.at[z], (jnp.maximum(z - 1, 0) * 2 + x, col))
    own_side = remote(v_ref, basis.at[z, x], x_send.at[z], x_recv.at[z], x_peer)

    @pl.when(z < 3)
    def _():
        own_up.start()

    @pl.when(z > 0)
    def _():
        own_down.start()

    own_side.start()
    basis[z, x] = v_ref[...]

    def build(i, carry):
        slot = lax.rem(i, 2)
        for copy in load(i, slot):
            copy.wait()
        here = pl.ds(pl.multiple_of(i * tile, tile), tile)
        buf[here, :] = (m_tile[slot].astype(F32) + g_tile[slot].astype(F32)).astype(BF16)

        @pl.when(i + 2 < tiles)
        def _():
            for copy in load(i + 2, slot):
                copy.start()

        return carry

    lax.fori_loop(0, tiles, build, 0)
    store = pltpu.make_async_copy(buf, b_hbm, store_sem)
    store.start()

    def hop(s):
        q = order[s]
        target = jnp.where(z == 1, jnp.where(q < z, 2, 0), jnp.where(q < z, 3, 1))
        return remote(basis.at[q, x], basis.at[q, x], hop_send.at[s - 1], z_recv.at[q], (target * 2 + x, col))

    def side(s):
        q = order[s]
        return remote(basis.at[q, x], basis.at[q, x], x_send.at[q], x_recv.at[q], x_peer)

    def take(s):
        hop(s).wait_recv()

        @pl.when(middle)
        def _():
            hop(s).start()

        side(s).start()

    def side_in(s):
        q = order[s]
        remote(basis.at[q, x], basis.at[q, 1 - x], x_send.at[q], x_recv.at[q], x_peer).wait_recv()

    wide = rows // 2

    def to_core(s, h):
        here = pl.ds(h * wide, wide)
        return remote(
            part.at[s, 1 - k, :, here], core_in.at[s, :, here], core_send.at[s, h], core_recv.at[s, h], core_peer
        )

    def to_y(s, h):
        here = pl.ds(h * wide, wide)
        return remote(half.at[s, :, here], y_in.at[s, :, here], y_send.at[s, h], y_recv.at[s, h], y_peer)

    def share(s, h):
        here = pl.ds(h * wide, wide)
        spot = pt_ref.at[order[s], k, :, here]
        return remote(spot, spot, share_send.at[s, h], share_recv.at[s, h], core_peer)

    def share_in(s, h):
        here = pl.ds(h * wide, wide)
        return remote(
            pt_ref.at[order[s], k, :, here], pt_ref.at[order[s], 1 - k, :, here],
            share_send.at[s, h], share_recv.at[s, h], core_peer,
        )

    def multiply(s):
        q = order[s]
        width = 512
        for h in range(2):

            def columns(n, carry):
                here = pl.ds(pl.multiple_of(n * width, width), width)
                left = basis[q].reshape(2 * basis.shape[2], basis.shape[3])
                value = nt_dot(left, buf[here, :])
                part[s, :, :, here] = value.astype(BF16).reshape(2, basis.shape[2], width)
                return carry

            lax.fori_loop(h * (wide // width), (h + 1) * (wide // width), columns, 0)
            to_core(s, h).start()

    def add_core(s):
        for h in range(2):
            here = slice(h * wide, (h + 1) * wide)
            to_core(s, h).wait_recv()
            half[s, :, here] = (part[s, k, :, here].astype(F32) + core_in[s, :, here].astype(F32)).astype(BF16)
            to_y(s, h).start()

    def add_y(s):
        for h in range(2):
            here = slice(h * wide, (h + 1) * wide)
            to_y(s, h).wait_recv()
            pt_ref[order[s], k, :, here] = (half[s, :, here].astype(F32) + y_in[s, :, here].astype(F32)).astype(BF16)
            share(s, h).start()

    take(1)

    @pl.when(middle)
    def _():
        take(2)

    side_in(0)
    multiply(0)

    @pl.when(jnp.logical_not(middle))
    def _():
        take(2)

    add_core(0)

    @pl.when(middle)
    def _():
        take(3)

    side_in(1)
    multiply(1)
    add_y(0)
    add_core(1)

    @pl.when(jnp.logical_not(middle))
    def _():
        take(3)

    side_in(2)
    multiply(2)
    add_y(1)
    add_core(2)
    side_in(3)
    multiply(3)
    add_y(2)
    add_core(3)
    add_y(3)

    @pl.when(z < 3)
    def _():
        own_up.wait_send()

    @pl.when(z > 0)
    def _():
        own_down.wait_send()

    own_side.wait_send()

    @pl.when(middle)
    def _():
        for s in range(1, 4):
            hop(s).wait_send()

    for s in range(1, 4):
        side(s).wait_send()
    for s in range(4):
        for h in range(2):
            to_core(s, h).wait_send()
            to_y(s, h).wait_send()
            share(s, h).wait_send()
            share_in(s, h).wait_recv()
    store.wait()


def project(v, m, g):
    rows, columns = m.shape
    ranks = v.shape[0]
    dma = pltpu.SemaphoreType.DMA
    vmem = pl.BlockSpec(memory_space=pltpu.VMEM)
    anywhere = pl.BlockSpec(memory_space=pl.ANY)
    return pl.pallas_call(
        project_kernel,
        out_shape=(
            jax.ShapeDtypeStruct((4, 2, ranks, rows), BF16),
            jax.ShapeDtypeStruct((rows, columns), BF16),
        ),
        in_specs=[vmem, anywhere, anywhere],
        out_specs=(vmem, anywhere),
        scratch_shapes=[
            pltpu.VMEM((rows, columns), BF16),
            pltpu.VMEM((4, 2, ranks, columns), BF16),
            pltpu.VMEM((2, 128, columns), BF16),
            pltpu.VMEM((2, 128, columns), BF16),
            pltpu.VMEM((4, 2, ranks, rows), BF16),
            pltpu.VMEM((4, ranks, rows), BF16),
            pltpu.VMEM((4, ranks, rows), BF16),
            pltpu.VMEM((4, ranks, rows), BF16),
            dma((2, 2)), dma, dma((2,)), dma((3,)), dma((4,)), dma((4,)), dma((4,)),
            dma((4, 2)), dma((4, 2)), dma((4, 2)), dma((4, 2)), dma((4, 2)), dma((4, 2)),
        ],
        compiler_params=pltpu.CompilerParams(
            collective_id=1, has_side_effects=True, vmem_limit_bytes=58 * 1024 * 1024
        ),
        cost_estimate=pl.CostEstimate(flops=2 * rows * columns * ranks * 8, bytes_accessed=6 * rows * columns, transcendentals=0),
        name="project",
    )(v, m, g)


def factor_kernel(
    pt_ref, b_hbm, o_ref, n_hbm, m_hbm, sums_ref,
    buf, wpart, x_in, z_in, whole, stack, stack_in, stack_all, work, inverse, squares, norm_in,
    load_sem, store_sem, back_sem, xs, xr, zs, zr, gs, gr, fs, ys,
    ss, sr, ts, tr, us, ur, ns, nr,
):
    row, col, z, x, y, k = places()
    ranks = pt_ref.shape[2]
    rank = work.shape[0]
    blocks = rank // BLOCK
    chunks = wpart.shape[0]
    width = wpart.shape[4]
    slice_rows = stack_in.shape[1]
    x_peer = (z * 2 + 1 - x, col)
    core_peer = (row, y * 2 + 1 - k)
    y_peer = (row, (1 - y) * 2 + k)

    def z_of(shift):
        return lax.rem(z + shift, 4)

    def z_peer(shift):
        return (z_of(shift) * 2 + x, col)

    def row_of(shift):
        return lax.rem(row + shift, 8)

    def load(j):
        return pltpu.make_async_copy(
            b_hbm.at[:, pl.ds(j * width, width)], buf.at[j % 2], load_sem.at[j % 2]
        )

    load(0).start()
    load(1).start()
    greet([(row_of(shift), col) for shift in range(1, 8)] + [core_peer, y_peer])

    def gram(t, carry):
        early = t < 8 - col
        i = jnp.where(early, col + t, t - 1)
        j = jnp.where(early, col, 7 - col)
        value = nt_dot(pt_ref[i // 2, lax.rem(i, 2)], pt_ref[j // 2, lax.rem(j, 2)])
        stack[pl.ds(pl.multiple_of(t * BLOCK, BLOCK), BLOCK), :] = value
        return carry

    lax.fori_loop(0, STACK, gram, 0)

    def part_of(r):
        return pl.ds(pl.multiple_of(r * slice_rows, slice_rows), slice_rows)

    def gram_out(shift):
        to = row_of(shift)
        return remote(stack.at[part_of(to)], stack_in.at[row], ss.at[shift], sr.at[row], (to, col))

    def gram_in(shift):
        who = row_of(shift)
        return remote(stack.at[part_of(row)], stack_in.at[who], ss.at[shift], sr.at[who], (who, col))

    def sum_out(shift):
        to = row_of(shift)
        return remote(stack_all.at[col, part_of(row)], stack_all.at[col, part_of(row)], ts.at[shift], tr.at[row], (to, col))

    def sum_in(shift):
        who = row_of(shift)
        return remote(stack_all.at[col, part_of(who)], stack_all.at[col, part_of(who)], ts.at[shift], tr.at[who], (who, col))

    def spread(index, what, device):
        return remote(stack_all.at[what], stack_all.at[what], us.at[index], ur.at[index], device)

    for shift in range(1, 8):
        gram_out(shift).start()

    def side_out(j):
        return remote(wpart.at[j, :, 1 - x], x_in.at[j], xs.at[j], xr.at[j], x_peer)

    def weigh(j, which):
        step = 256

        def columns(n, carry):
            here = pl.ds(pl.multiple_of(n * step, step), step)
            left = pt_ref[:, which].reshape(4 * ranks, pt_ref.shape[3])
            value = jnp.dot(left, buf[j % 2, :, here], preferred_element_type=F32)
            wpart[j, :, which, :, here] = value.astype(BF16).reshape(4, ranks, step)
            return carry

        lax.fori_loop(0, width // step, columns, 0)

    def product(j):
        load(j).wait()
        weigh(j, 1 - x)
        if j < 1:
            side_out(j).start()
        weigh(j, x)
        if j + 2 < chunks:
            load(j + 2).start()

    end = jnp.logical_or(z == 0, z == 3)
    low = z < 2

    def line_send(j, i, piece, to, slot):
        return remote(x_in.at[j, piece], z_in.at[j, slot], zs.at[j, i], zr.at[j, slot], (to * 2 + x, col))

    def line_take(j, slot):
        remote(x_in.at[j, 0], z_in.at[j, slot], zs.at[j, 0], zr.at[j, slot], x_peer).wait_recv()

    def line_first(j):
        for i in range(3):
            piece = jnp.where(low, 3 - i, i)
            slot = piece if i < 2 else jnp.where(low, 1, 4)
            line_send(j, i, piece, jnp.where(low, 1, 2), slot).start()

    def add_in(j, piece):
        line_take(j, piece)
        x_in[j, piece] = (x_in[j, piece].astype(F32) + z_in[j, piece].astype(F32)).astype(BF16)

    def add_side(j):
        side_out(j).wait_recv()
        if j + 1 < chunks:
            side_out(j + 1).start()
        for shift in (1, 2, 3, 0):
            there = z_of(shift)
            x_in[j, there] = (wpart[j, there, x].astype(F32) + x_in[j, there].astype(F32)).astype(BF16)

        @pl.when(end)
        def _():
            line_first(j)

    def line_second(j):
        @pl.when(jnp.logical_not(end))
        def _():
            for i in range(2):
                piece = jnp.where(low, 3 - i, i)
                slot = piece if i < 1 else jnp.where(low, 2, 4)
                add_in(j, piece)
                line_send(j, i, piece, jnp.where(low, 2, 1), slot).start()

    def line_third(j):
        @pl.when(jnp.logical_not(end))
        def _():
            piece = jnp.where(low, 0, 3)
            add_in(j, piece)
            line_send(j, 2, piece, piece, jnp.where(low, 4, 3)).start()

    order = [z, jnp.bitwise_xor(z, 1), jnp.where(low, 2, 1), jnp.where(low, 3, 0)]

    def full_send(j, q, sem, to):
        return remote(whole.at[j, q, x], whole.at[j, q, x], gs.at[j, sem], gr.at[j, q], (to * 2 + x, col))

    def own_up(j):
        return full_send(j, z, 0, jnp.minimum(z + 1, 3))

    def own_down(j):
        return full_send(j, z, 1, jnp.maximum(z - 1, 0))

    def hop(j, s):
        q = order[s]
        return full_send(j, q, s + 1, jnp.where(low, jnp.where(q < z, 2, 0), jnp.where(q < z, 3, 1)))

    def full_side(j, q):
        return remote(whole.at[j, q, x], whole.at[j, q, x], fs.at[j, q], ys.at[j, q], x_peer)

    def full_side_in(j, q):
        return remote(whole.at[j, q, x], whole.at[j, q, 1 - x], fs.at[j, q], ys.at[j, q], x_peer)

    def finish(j):
        @pl.when(z > 0)
        def _():
            line_take(j, z)
            x_in[j, z] = (x_in[j, z].astype(F32) + z_in[j, z].astype(F32)).astype(BF16)

        @pl.when(z < 3)
        def _():
            line_take(j, 4)
            x_in[j, z] = (x_in[j, z].astype(F32) + z_in[j, 4].astype(F32)).astype(BF16)

        whole[j, z, x] = x_in[j, z]

        @pl.when(z < 3)
        def _():
            own_up(j).start()

        @pl.when(z > 0)
        def _():
            own_down(j).start()

        full_side(j, z).start()

    def take(j, s):
        hop(j, s).wait_recv()

        @pl.when(jnp.logical_not(end))
        def _():
            hop(j, s).start()

        full_side(j, order[s]).start()

    def take_first(j):
        take(j, 1)

        @pl.when(jnp.logical_not(end))
        def _():
            take(j, 2)

    def take_second(j):
        @pl.when(end)
        def _():
            take(j, 2)

    def take_third(j):
        take(j, 3)

    def sum_gram():
        total = stack[part_of(row), :]
        for shift in range(1, 8):
            gram_in(shift).wait_recv()
            total = total + stack_in[row_of(shift)]
        stack_all[col, part_of(row), :] = total
        for shift in range(1, 8):
            sum_out(shift).start()

    other_col = (1 - y) * 2 + k

    def spread_gram():
        for shift in range(1, 8):
            sum_in(shift).wait_recv()
        spread(1, col, y_peer).start()
        spread(0, col, core_peer).start()

    def end_gram():
        spread(1, other_col, y_peer).wait_recv()
        spread(2, other_col, core_peer).start()
        spread(0, y * 2 + 1 - k, core_peer).wait_recv()
        spread(2, (1 - y) * 2 + 1 - k, core_peer).wait_recv()

    product(0)
    product(1)
    product(2)
    sum_gram()
    product(3)
    add_side(0)
    spread_gram()
    line_second(0)
    end_gram()

    for c in range(4):
        for t in range(STACK):
            i, j = (c + t, c) if t < 8 - c else (t - 1, 7 - c)
            value = stack_all[c, BLOCK * t : BLOCK * (t + 1), :]
            work[BLOCK * i : BLOCK * (i + 1), BLOCK * j : BLOCK * (j + 1)] = value
            if i != j:
                work[BLOCK * j : BLOCK * (j + 1), BLOCK * i : BLOCK * (i + 1)] = value.T

    column_block = lax.broadcasted_iota(jnp.int32, (BLOCK, rank), 1) // BLOCK
    events = {
        0: [(add_side, 1), (line_third, 0)],
        1: [(finish, 0), (line_second, 1)],
        2: [(add_side, 2), (line_third, 1)],
        3: [(take_first, 0), (finish, 1)],
        4: [(line_second, 2), (take_second, 0)],
        5: [(add_side, 3), (line_third, 2), (take_third, 0), (take_first, 1)],
        6: [(finish, 2), (line_second, 3)],
        7: [(take_second, 1), (line_third, 3), (take_third, 1)],
    }

    def step(kk, carry):
        here = pl.ds(pl.multiple_of(kk * BLOCK, BLOCK), BLOCK)
        factor = factor_block(work[here, here])
        pivot_rows = jnp.dot(factor, work[here, :], precision=HIGHEST, preferred_element_type=F32)
        wide = jnp.concatenate([factor] * blocks, axis=1)
        pivot_rows = jnp.where(column_block == kk, wide, pivot_rows)
        work[here, :] = pivot_rows

        def below(i, carry):
            there = pl.ds(pl.multiple_of(i * BLOCK, BLOCK), BLOCK)
            panel = lax.dot_general(
                work[there, here], factor, (((1,), (1,)), ((), ())),
                precision=HIGHEST, preferred_element_type=F32,
            )
            work[there, here] = jnp.zeros((BLOCK, BLOCK), F32)
            work[there, :] = work[there, :] - jnp.dot(
                panel, work[here, :], precision=HIGHEST, preferred_element_type=F32
            )
            return carry

        lax.fori_loop(kk + 1, blocks, below, 0)
        rest = jnp.where(column_block <= kk, pivot_rows, 0.0)
        high = rest.astype(BF16)
        inverse[0, here, :] = high
        inverse[1, here, :] = (rest - high.astype(F32)).astype(BF16)
        for at, todo in events.items():
            if todo:
                @pl.when(kk == at)
                def _(todo=todo):
                    for function, j in todo:
                        function(j)
        return carry

    lax.fori_loop(0, blocks, step, 0)

    def apply(load_right, store_out, columns):
        tile = 512

        def one(n, carry):
            here = pl.ds(pl.multiple_of(n * tile, tile), tile)
            right = load_right(here)
            for i in range(4):
                rows = slice(256 * i, 256 * (i + 1))
                deep = 256 * (i + 1)
                left = inverse[:, rows, :deep].reshape(512, deep)
                value = jnp.dot(left, right[:deep], preferred_element_type=F32)
                store_out(i, here, value[:256] + value[256:])
            return carry

        lax.fori_loop(0, columns // tile, one, 0)

    def p_load(here):
        return pt_ref[:, :, :, here].reshape(rank, 512)

    def o_store(i, here, value):
        o_ref[here, 256 * i : 256 * (i + 1)] = value.T.astype(BF16)

    load(0).start()
    load(1).start()
    finish(3)
    take_first(2)
    apply(p_load, o_store, pt_ref.shape[3])
    squares[...] = jnp.zeros_like(squares)

    def store(j):
        return pltpu.make_async_copy(
            wpart.at[j], n_hbm.at[:, :, :, pl.ds(j * width, width)], store_sem.at[j]
        )

    def back(j):
        return pltpu.make_async_copy(
            buf.at[j % 2], m_hbm.at[:, pl.ds(j * width, width)], back_sem.at[j % 2]
        )

    def right(j):
        for q in range(4):
            full_side_in(j, q).wait_recv()
        side_out(j).wait_send()

        def w_load(here):
            return whole[j, :, :, :, here].reshape(rank, 512)

        def n_store(i, here, value):
            low = value.astype(BF16)
            wpart[j, i, :, :, here] = low.reshape(2, ranks, 512)
            low = low.astype(F32)
            low = low * low
            squares[256 * i : 256 * (i + 1), :] += sum(
                low[:, BLOCK * g : BLOCK * (g + 1)] for g in range(1, 4)
            ) + low[:, :BLOCK]

        apply(w_load, n_store, width)
        store(j).start()

    def feed_back(j):
        load(j).wait()
        tall, wide = 512, 512

        def one(t, carry):
            across_tiles = width // wide
            rows = pl.ds(pl.multiple_of(t // across_tiles * tall, tall), tall)
            here = pl.ds(pl.multiple_of(lax.rem(t, across_tiles) * wide, wide), wide)
            value = jnp.dot(
                o_ref[rows, :], wpart[j, :, :, :, here].reshape(rank, wide), preferred_element_type=F32
            )
            old = buf[j % 2, rows, here].astype(F32)
            buf[j % 2, rows, here] = (old - (1.0 - momentum_decay) * value).astype(BF16)
            return carry

        lax.fori_loop(0, buf.shape[1] // tall * (width // wide), one, 0)
        back(j).start()

    def refill(j):
        back(j).wait()
        load(j + 2).start()

    take_second(2)
    right(0)
    take_third(2)
    take_first(3)
    feed_back(0)
    take_second(3)
    right(1)
    refill(0)
    take_third(3)
    feed_back(1)
    right(2)
    refill(1)
    feed_back(2)
    right(3)

    def norm(shift):
        to = lax.rem(col + shift, 4)
        return remote(norm_in.at[col], norm_in.at[col], ns.at[shift], nr.at[col], (row, to))

    def norm_from(shift):
        who = lax.rem(col + shift, 4)
        return remote(norm_in.at[who], norm_in.at[who], ns.at[shift], nr.at[who], (row, who))

    ones = jnp.ones((GROUP, BLOCK), F32)
    norm_in[col] = lax.dot_general(
        ones, squares[...], (((1,), (1,)), ((), ())), precision=HIGHEST, preferred_element_type=F32
    )
    for shift in range(1, 4):
        norm(shift).start()
    feed_back(3)
    for shift in range(1, 4):
        norm_from(shift).wait_recv()
    sums_ref[...] = (norm_in[0] + norm_in[1]) + (norm_in[2] + norm_in[3])
    for shift in range(1, 4):
        norm(shift).wait_send()
    for shift in range(1, 8):
        gram_out(shift).wait_send()
        sum_out(shift).wait_send()
    spread(0, col, core_peer).wait_send()
    spread(1, col, y_peer).wait_send()
    spread(2, other_col, core_peer).wait_send()
    for j in range(chunks):
        for i in range(3):
            line_send(j, i, 0, z, 0).wait_send()

        @pl.when(z < 3)
        def _():
            own_up(j).wait_send()

        @pl.when(z > 0)
        def _():
            own_down(j).wait_send()

        @pl.when(jnp.logical_not(end))
        def _():
            for s in range(1, 4):
                hop(j, s).wait_send()

        for q in range(4):
            full_side(j, q).wait_send()
        store(j).wait()
    back(chunks - 2).wait()
    back(chunks - 1).wait()


def factorize(pt, b):
    _, _, ranks, rows = pt.shape
    columns = b.shape[1]
    rank = 8 * ranks
    width = columns // CHUNKS
    slice_rows = STACK * BLOCK // 8
    dma = pltpu.SemaphoreType.DMA
    vmem = pl.BlockSpec(memory_space=pltpu.VMEM)
    anywhere = pl.BlockSpec(memory_space=pl.ANY)
    return pl.pallas_call(
        factor_kernel,
        out_shape=(
            jax.ShapeDtypeStruct((rows, rank), BF16),
            jax.ShapeDtypeStruct((4, 2, ranks, columns), BF16),
            jax.ShapeDtypeStruct((rows, columns), BF16),
            jax.ShapeDtypeStruct((GROUP, rank), F32),
        ),
        in_specs=[vmem, anywhere],
        out_specs=(vmem, anywhere, anywhere, vmem),
        scratch_shapes=[
            pltpu.VMEM((2, rows, width), BF16),
            pltpu.VMEM((CHUNKS, 4, 2, ranks, width), BF16),
            pltpu.VMEM((CHUNKS, 4, ranks, width), BF16),
            pltpu.VMEM((CHUNKS, 5, ranks, width), BF16),
            pltpu.VMEM((CHUNKS, 4, 2, ranks, width), BF16),
            pltpu.VMEM((STACK * BLOCK, BLOCK), F32),
            pltpu.VMEM((8, slice_rows, BLOCK), F32),
            pltpu.VMEM((4, STACK * BLOCK, BLOCK), F32),
            pltpu.VMEM((rank, rank), F32),
            pltpu.VMEM((2, rank, rank), BF16),
            pltpu.VMEM((rank, BLOCK), F32),
            pltpu.VMEM((4, GROUP, rank), F32),
            dma((2,)), dma((CHUNKS,)), dma((2,)), dma((CHUNKS,)), dma((CHUNKS,)),
            dma((CHUNKS, 3)), dma((CHUNKS, 5)), dma((CHUNKS, 5)), dma((CHUNKS, 4)),
            dma((CHUNKS, 4)), dma((CHUNKS, 4)),
            dma((8,)), dma((8,)), dma((8,)), dma((8,)), dma((3,)), dma((3,)), dma((4,)), dma((4,)),
        ],
        compiler_params=pltpu.CompilerParams(
            collective_id=2, has_side_effects=True, vmem_limit_bytes=58 * 1024 * 1024
        ),
        name="factorize",
    )(pt, b)


def update_kernel(o_ref, n_ref, m_ref, sums_ref, m_out, basis_ref, update_ref, inverse, left):
    ranks = basis_ref.shape[0]
    rows = o_ref.shape[0]
    pieces = 4
    tall = rows // pieces

    @pl.when(pl.program_id(0) == 0)
    def _():
        norm = lax.rsqrt(sums_ref[0:1, :] + epsilon)
        inverse[...] = jnp.broadcast_to(norm, (BLOCK, norm.shape[1])).T
        scale = D / math.sqrt(RANK) * norm
        for i in range(pieces):
            part = slice(i * tall, (i + 1) * tall)
            left[part, :] = (o_ref[part, :].astype(F32) * scale).astype(BF16)

    width = n_ref.shape[1]
    mine = pl.ds(pl.multiple_of(lax.axis_index("row") * ranks, ranks), ranks)
    own = jnp.concatenate([inverse[mine, :]] * (width // BLOCK), axis=1)
    basis_ref[...] = n_ref[mine, :].astype(F32) * own
    for i in range(pieces):
        part = slice(i * tall, (i + 1) * tall)
        update_ref[part, :] = jnp.dot(
            left[part, :], n_ref[...], preferred_element_type=F32
        ).astype(BF16)
        m_out[part, :] = m_ref[part, :]


def finish_update(ortho, right_new, momentum_next, sums, ranks):
    rows, columns = momentum_next.shape
    rank = ortho.shape[1]
    width = 512

    def strip(height):
        return pl.BlockSpec((height, width), lambda j: (0, j))

    def fixed(shape):
        return pl.BlockSpec(shape, lambda j: (0, 0))

    return pl.pallas_call(
        update_kernel,
        grid=(columns // width,),
        out_shape=(
            jax.ShapeDtypeStruct((rows, columns), BF16),
            jax.ShapeDtypeStruct((ranks, columns), F32),
            jax.ShapeDtypeStruct((rows, columns), BF16),
        ),
        in_specs=[fixed((rows, rank)), strip(rank), strip(rows), fixed((GROUP, rank))],
        out_specs=(strip(rows), strip(ranks), strip(rows)),
        scratch_shapes=[
            pltpu.VMEM((rank, BLOCK), F32),
            pltpu.VMEM((rows, rank), BF16),
        ],
        compiler_params=pltpu.CompilerParams(vmem_limit_bytes=58 * 1024 * 1024),
        cost_estimate=pl.CostEstimate(flops=2 * rows * columns * rank, bytes_accessed=8 * rows * columns, transcendentals=0),
        name="update",
    )(ortho, right_new, momentum_next, sums)


def body(momentum, gradient, right_basis):
    pt, buffer = project(right_basis, momentum, gradient)
    ortho, right_new, momentum_next, sums = factorize(pt, buffer)
    right_new = right_new.reshape(ortho.shape[1], buffer.shape[1])
    return finish_update(ortho, right_new, momentum_next, sums, right_basis.shape[0])


def solution(mesh):
    sizes = (mesh.shape["row"], mesh.shape["col"])
    return jax.shard_map(
        body if sizes == (8, 4) else plain_body,
        mesh=mesh,
        in_specs=(P("row", "col"), P("row", "col"), P("row", "col")),
        out_specs=(P("row", "col"), P("row", "col"), P("row", "col")),
        check_vma=False,
    )
```
